32 devices in a mesh: ep: 16 (over z, y, x), tp: 2 (over core).
Axes of the slice: x: 2, y: 2, z: 4, core: 2. Of those that a mesh axis runs over, the one named last changes fastest.
Arguments:
- tokens: bfloat16 [4096, 4096], P(('ep', 'tp')), may hold values from -6 to 6
- expert_ids: int32 [4096, 8], P(('ep', 'tp')), may hold values from 0 to 127, as said below
- gate_weights: float32 [4096, 8], P(('ep', 'tp')), may hold values from 0.1 to 1
- grad_out: bfloat16 [4096, 4096], P(('ep', 'tp')), may hold values from -6 to 6
- w_gate: bfloat16 [16, 768, 4096], P('ep', 'tp'), may hold values from -0.09375 to 0.09375
- w_up: bfloat16 [16, 768, 4096], P('ep', 'tp'), may hold values from -0.09375 to 0.09375
- w_down: bfloat16 [16, 768, 4096], P('ep', 'tp'), may hold values from -0.21875 to 0.21875
Outputs:
- grad_tokens: bfloat16 [4096, 4096], P(('ep', 'tp'))
- grad_gate: bfloat16 [16, 768, 4096], P('ep', 'tp')
- grad_up: bfloat16 [16, 768, 4096], P('ep', 'tp')
- grad_down: bfloat16 [16, 768, 4096], P('ep', 'tp')
The draws below stay inside these ranges and needn't reach their ends.
Inputs may be any that keep to these rules, and one draw needn't show every extreme that they name: `expert_ids`: each token names 8 different experts. No expert below 16 is named by more than 8 tokens of one device's rows, and in every draw some expert below 16 is named by exactly 8 tokens of every device's rows.
All inputs are finite; a program needn't handle non-finite values.
Results may differ from the reference program's by a relative error of at most 0.0064.
Values may be sent and summed in bfloat16 or wider, within the bound.
No kernel may reach another device: no remote copies, remote signals or barrier semaphores. Data moves between devices by JAX's collectives and lax.ppermute only.
A program may use at most 192 MiB of HBM per device.

```python
import math
import jax
import jax.numpy as jnp
from jax import lax

D = 4096
FF = 768
ALL_EXPERTS = 128
TOPK = 8
TOK_DEV = 128
WIN = 16
CAP = 8
TOKENS = 4096
N_EP = 16
N_TP = 2


def draw_expert_ids(key, part):
    blocks = TOKENS // TOK_DEV
    per_class = WIN // TOPK
    outside = ALL_EXPERTS // TOPK - per_class
    keys = jax.random.split(jax.random.fold_in(key, 17), 4)
    ranking = jax.vmap(lambda inner: jax.random.permutation(inner, per_class))(jax.random.split(keys[0], TOPK))
    base_load = CAP // (1 + ranking)
    noise = jax.random.randint(keys[1], (blocks, TOPK, per_class), 0, CAP // 2 + 1)
    loads = jnp.minimum(base_load[None, :, :] + noise, CAP)
    ends = jnp.cumsum(loads, axis=2)
    totals = ends[:, :, -1]
    order = jax.vmap(lambda inner: jax.random.permutation(inner, TOK_DEV))(jax.random.split(keys[2], blocks * TOPK))
    order = order.reshape(blocks, TOPK, TOK_DEV)
    inside = jnp.sum((order[:, :, :, None] >= ends[:, :, None, :]).astype(jnp.int32), axis=3)
    valid = order < totals[:, :, None]
    away = per_class + jax.random.randint(keys[3], (blocks, TOPK, TOK_DEV), 0, outside)
    column = jnp.where(valid, inside, away)
    classes = jnp.arange(TOPK, dtype=jnp.int32)
    ids = classes[None, :, None] + TOPK * column
    return jnp.transpose(ids, (0, 2, 1)).reshape(TOKENS, TOPK).astype(jnp.int32)


def level_of(own_key, shape, pieces, smallest, largest):
    def one(axis_at, parts):
        steps = jax.random.uniform(jax.random.fold_in(jax.random.fold_in(own_key, 6), axis_at), (parts,), jnp.float32, smallest / len(pieces), largest / len(pieces))
        return jnp.repeat(jnp.exp(steps), shape[axis_at] // parts).reshape((-1,) + (1,) * (len(shape) - axis_at - 1))

    loudness = one(*pieces[0])
    for cut in pieces[1:]:
        loudness = loudness * one(*cut)
    return loudness


def centred(own_key, dims, width, reach, cuts=(), held_as=jnp.bfloat16):
    array = width * jax.random.normal(own_key, dims, jnp.float32)
    if cuts:
        array = array * level_of(own_key, dims, cuts, -0.22, 0.18)
    return jnp.clip(array, -reach, reach).astype(held_as)


def setup_inputs(seed: int = 0) -> dict:
    key_list = jax.random.split(jax.random.key(seed), 8)
    return {
        "tokens": centred(key_list[0], (TOKENS, D), 1.0, 6.0, ((0, 32),)),
        "expert_ids": draw_expert_ids(jax.random.fold_in(key_list[7], 71), 0),
        "gate_weights": jnp.clip(jnp.exp(math.log(1.0) - 2.3025851 * jax.random.uniform(key_list[2], (TOKENS, TOPK), jnp.float32) ** level_of(key_list[2], (TOKENS, TOPK), ((0, 32),), -0.2, 0.2)), 0.1, 1.0),
        "grad_out": centred(key_list[3], (TOKENS, D), 1.0, 6.0, ((0, 32),)),
        "w_gate": centred(key_list[4], (WIN, FF, D), D ** -0.5, 0.09375, ((0, 16), (1, 2))),
        "w_up": centred(key_list[5], (WIN, FF, D), D ** -0.5, 0.09375, ((0, 16), (1, 2))),
        "w_down": centred(key_list[6], (WIN, FF, D), FF ** -0.5, 0.21875, ((0, 16), (1, 2))),
    }


def expert_terms(rows_x, rows_dy, gate_rows, up_rows, down_rows):
    contract_last = (((1,), (1,)), ((), ()))
    contract_first = (((0,), (0,)), ((), ()))
    pre_gate = lax.dot_general(rows_x, gate_rows, contract_last, preferred_element_type=jnp.float32)
    pre_up = lax.dot_general(rows_x, up_rows, contract_last, preferred_element_type=jnp.float32)
    sigmoid_gate = jax.nn.sigmoid(pre_gate)
    activated = (pre_gate * sigmoid_gate * pre_up).astype(jnp.bfloat16)
    d_act = lax.dot_general(rows_dy, down_rows, contract_last, preferred_element_type=jnp.float32)
    d_up = (d_act * pre_gate * sigmoid_gate).astype(jnp.bfloat16)
    d_pre = (d_act * pre_up * sigmoid_gate * (1.0 + pre_gate * (1.0 - sigmoid_gate))).astype(jnp.bfloat16)
    grad_gate = lax.dot_general(d_pre, rows_x, contract_first, preferred_element_type=jnp.float32)
    grad_up = lax.dot_general(d_up, rows_x, contract_first, preferred_element_type=jnp.float32)
    grad_down = lax.dot_general(activated, rows_dy, contract_first, preferred_element_type=jnp.float32)
    return grad_gate, grad_up, grad_down, d_pre, d_up


def reference(tokens, expert_ids, gate_weights, grad_out, w_gate, w_up, w_down):
    most = N_EP * N_TP * CAP

    def per_expert(packed):
        expert, gate_rows, up_rows, down_rows = packed
        hit = expert_ids == expert
        member = jnp.any(hit, axis=1)
        gate = jnp.sum(jnp.where(hit, gate_weights, jnp.zeros((), jnp.float32)), axis=1)
        chosen = jnp.argsort(jnp.where(member, 0, 1).astype(jnp.int32), stable=True)[:most].astype(jnp.int32)
        live = member[chosen]
        rows_x = jnp.where(live[:, None], tokens[chosen], jnp.zeros((), tokens.dtype))
        scaled = (gate[chosen][:, None] * grad_out[chosen].astype(jnp.float32)).astype(jnp.bfloat16)
        rows_dy = jnp.where(live[:, None], scaled, jnp.zeros((), scaled.dtype))
        grad_gate, grad_up, grad_down, d_pre, d_up = expert_terms(rows_x, rows_dy, gate_rows, up_rows, down_rows)
        row_grad = (jnp.dot(d_pre, gate_rows, preferred_element_type=jnp.float32)
                    + jnp.dot(d_up, up_rows, preferred_element_type=jnp.float32)).astype(jnp.bfloat16)
        row_grad = jnp.where(live[:, None], row_grad, jnp.zeros((), row_grad.dtype))
        return (grad_gate.astype(jnp.bfloat16), grad_up.astype(jnp.bfloat16),
                grad_down.astype(jnp.bfloat16), row_grad, chosen)

    grad_gate, grad_up, grad_down, row_grad, chosen = lax.map(
        per_expert, (jnp.arange(WIN, dtype=jnp.int32), w_gate, w_up, w_down))
    total = jnp.zeros((TOKENS, D), jnp.float32).at[chosen.reshape(-1)].add(
        row_grad.reshape(-1, D).astype(jnp.float32))
    return total.astype(jnp.bfloat16), grad_gate, grad_up, grad_down
```

```python
import functools

import jax
import jax.numpy as jnp
from jax import lax
from jax.experimental import pallas as pl
from jax.experimental.pallas import tpu as pltpu
from jax.sharding import PartitionSpec as P

CAP = 8
HALF = CAP // 2
VMEM_LIMIT = 60 * 1024 * 1024

f32 = jnp.float32
bf16 = jnp.bfloat16


def low_rows(shape):
    return (lax.broadcasted_iota(jnp.int32, shape, 0) & HALF) == 0


def gather_kernel(chunk, experts, ids_ref, gates_ref, tok_ref, dy_ref, send_ref, match_ref, gate_s):
    rows, count = match_ref.shape
    topk = ids_ref.shape[0]

    @pl.when(pl.program_id(0) == 0)
    def _():
        expert_at = lax.broadcasted_iota(jnp.int32, (experts, count), 0)
        member = jnp.zeros((experts, count), f32)
        for k in range(topk):
            member += jnp.where(ids_ref[k : k + 1, :] == expert_at, 1.0, 0.0)
        earlier = jnp.where(
            lax.broadcasted_iota(jnp.int32, (count, count), 0)
            < lax.broadcasted_iota(jnp.int32, (count, count), 1),
            1.0,
            0.0,
        ).astype(bf16)
        before = jnp.dot(member.astype(bf16), earlier, preferred_element_type=f32)
        row = lax.broadcasted_iota(jnp.int32, (rows, count), 0)
        wanted = row - (row & HALF) + HALF * chunk
        match = jnp.zeros((rows, count), f32)
        gate = jnp.zeros((rows, count), f32)
        for k in range(topk):
            named = ids_ref[k : k + 1, :]
            place = jnp.sum(
                jnp.where(named == expert_at, before, 0.0), axis=0, keepdims=True
            ).astype(jnp.int32)
            target = jnp.where(named < experts, named * CAP + place, -1)
            hit = target == wanted
            match = jnp.where(hit, 1.0, match)
            gate = jnp.where(hit, gates_ref[k : k + 1, :], gate)
        match_ref[...] = match.astype(bf16)
        gate_s[...] = jnp.broadcast_to(jnp.sum(gate, axis=1, keepdims=True), gate_s.shape)

    match = match_ref[...]
    picked_x = jnp.dot(match, tok_ref[...], preferred_element_type=f32)
    picked_dy = jnp.dot(match, dy_ref[...], preferred_element_type=f32)
    out = jnp.where(low_rows(picked_x.shape), picked_x, gate_s[:, :1] * picked_dy)
    send_ref[...] = out.astype(bf16)


def gather(chunk, experts, ids, gates, tokens, grad_out):
    count, width = tokens.shape
    rows = experts * CAP
    block = width // 4
    whole = lambda i: (0, 0)
    return pl.pallas_call(
        functools.partial(gather_kernel, chunk, experts),
        grid=(width // block,),
        in_specs=[
            pl.BlockSpec(ids.shape, whole),
            pl.BlockSpec(gates.shape, whole),
            pl.BlockSpec((count, block), lambda i: (0, i)),
            pl.BlockSpec((count, block), lambda i: (0, i)),
        ],
        out_specs=[
            pl.BlockSpec((rows, block), lambda i: (0, i)),
            pl.BlockSpec((rows, count), whole),
        ],
        out_shape=[
            jax.ShapeDtypeStruct((rows, width), bf16),
            jax.ShapeDtypeStruct((rows, count), bf16),
        ],
        scratch_shapes=[pltpu.VMEM((rows, 128), f32)],
        name=f"gather_{chunk}",
        cost_estimate=pl.CostEstimate(
            flops=4 * rows * count * width, bytes_accessed=4 * width * (rows + count) * 2, transcendentals=0
        ),
        compiler_params=pltpu.CompilerParams(vmem_limit_bytes=VMEM_LIMIT),
    )(ids, gates, tokens, grad_out)


def expert_kernel(
    mine_ref, other_ref, gate_ref, up_ref, down_ref,
    own_ref, partner_ref, coef_ref,
    rows_s, joined_s, down_s, acc_s, fold_s, sems,
):
    blocks, both, block = rows_s.shape
    rows = both // 2
    hidden = down_s.shape[1]

    def copies(i):
        cols = pl.ds(pl.multiple_of(i * block, block), block)
        pairs = (
            (mine_ref.at[:, cols], rows_s.at[i, pl.ds(0, rows)]),
            (other_ref.at[:, cols], rows_s.at[i, pl.ds(rows, rows)]),
            (gate_ref.at[:, cols], joined_s.at[i, pl.ds(0, hidden)]),
            (up_ref.at[:, cols], joined_s.at[i, pl.ds(hidden, hidden)]),
            (down_ref.at[:, cols], down_s.at[i]),
        )
        return [pltpu.make_async_copy(a, b, sems.at[i, c]) for c, (a, b) in enumerate(pairs)]

    for i in range(blocks):
        for copy in copies(i):
            copy.start()

    contract_last = (((1,), (1,)), ((), ()))
    for i in range(blocks):
        for copy in copies(i):
            copy.wait()
        here = rows_s[i]
        first = lax.dot_general(here, joined_s[i], contract_last, preferred_element_type=f32)
        second = lax.dot_general(here, down_s[i], contract_last, preferred_element_type=f32)
        if i == 0:
            acc_s[:, : 2 * hidden] = first
            acc_s[:, 2 * hidden :] = second
        else:
            acc_s[:, : 2 * hidden] += first
            acc_s[:, 2 * hidden :] += second

    step = 64

    @pl.loop(0, both // step)
    def _(b):
        at = pl.ds(pl.multiple_of(b * step, step), step)
        low = low_rows((step, hidden))
        g = acc_s[at, :hidden]
        u = acc_s[at, hidden : 2 * hidden]
        a = acc_s[at, 2 * hidden :]
        g = jnp.where(low, g, pltpu.roll(g, HALF, axis=0))
        u = jnp.where(low, u, pltpu.roll(u, HALF, axis=0))
        a = jnp.where(low, pltpu.roll(a, step - HALF, axis=0), a)
        s = jax.nn.sigmoid(g)
        act = g * s * u
        d_up = a * g * s
        d_pre = a * u * s * (1.0 + g * (1.0 - s))
        zero = jnp.zeros_like(act)
        fold_s[at, :hidden] = d_pre.astype(bf16)
        fold_s[at, hidden:] = d_up.astype(bf16)
        coef_ref[at, :hidden] = jnp.where(low, d_pre, zero).astype(bf16)
        coef_ref[at, hidden : 2 * hidden] = jnp.where(low, d_up, zero).astype(bf16)
        coef_ref[at, 2 * hidden :] = jnp.where(low, zero, act).astype(bf16)

    low = low_rows((both, block))
    for i in range(blocks // 2):
        fold = fold_s[...]
        left = jnp.dot(fold, joined_s[i], preferred_element_type=f32)
        right = jnp.dot(fold, joined_s[i + blocks // 2], preferred_element_type=f32)
        out = jnp.where(low, left, right)
        own_ref[:, i * block : (i + 1) * block] = out[:rows]
        partner_ref[:, i * block : (i + 1) * block] = out[rows:].astype(bf16)


def expert_terms(mine, other, w_gate, w_up, w_down):
    rows, width = mine.shape
    hidden = w_gate.shape[0]
    blocks = 4
    block = width // blocks
    hbm = pl.BlockSpec(memory_space=pl.ANY)
    vmem = pl.BlockSpec(memory_space=pltpu.VMEM)
    return pl.pallas_call(
        expert_kernel,
        in_specs=[hbm] * 5,
        out_specs=[vmem] * 3,
        out_shape=[
            jax.ShapeDtypeStruct((rows, width // 2), f32),
            jax.ShapeDtypeStruct((rows, width // 2), bf16),
            jax.ShapeDtypeStruct((2 * rows, 3 * hidden), bf16),
        ],
        scratch_shapes=[
            pltpu.VMEM((blocks, 2 * rows, block), bf16),
            pltpu.VMEM((blocks, 2 * hidden, block), bf16),
            pltpu.VMEM((blocks, hidden, block), bf16),
            pltpu.VMEM((2 * rows, 3 * hidden), f32),
            pltpu.VMEM((2 * rows, 2 * hidden), bf16),
            pltpu.SemaphoreType.DMA((blocks, 5)),
        ],
        name="expert_terms",
        cost_estimate=pl.CostEstimate(
            flops=20 * rows * hidden * width,
            bytes_accessed=6 * hidden * width + 7 * rows * width,
            transcendentals=2 * rows * hidden,
        ),
        compiler_params=pltpu.CompilerParams(vmem_limit_bytes=VMEM_LIMIT),
    )(mine, other, w_gate, w_up, w_down)


def weight_kernel(coef_a, coef_b, mine_a, other_a, mine_b, other_b, gate_ref, up_ref, down_ref, turned):
    both = coef_a.shape[0]
    hidden = gate_ref.shape[0]

    @pl.when(pl.program_id(0) == 0)
    def _():
        turned[:, :both] = coef_a[...].T
        turned[:, both:] = coef_b[...].T

    rows = jnp.concatenate([mine_a[...], other_a[...], mine_b[...], other_b[...]], axis=0)
    for k, out in enumerate((gate_ref, up_ref, down_ref)):
        out[...] = jnp.dot(
            turned[k * hidden : (k + 1) * hidden, :], rows, preferred_element_type=f32
        ).astype(bf16)


def weight_grads(coef_a, coef_b, mine_a, other_a, mine_b, other_b):
    rows, width = mine_a.shape
    hidden = coef_a.shape[1] // 3
    block = 512
    whole = lambda i: (0, 0)
    cols = lambda i: (0, i)
    return pl.pallas_call(
        weight_kernel,
        grid=(width // block,),
        in_specs=[pl.BlockSpec(coef_a.shape, whole)] * 2 + [pl.BlockSpec((rows, block), cols)] * 4,
        out_specs=[pl.BlockSpec((hidden, block), cols)] * 3,
        out_shape=[jax.ShapeDtypeStruct((hidden, width), bf16)] * 3,
        scratch_shapes=[pltpu.VMEM((3 * hidden, 4 * rows), bf16)],
        name="weight_grads",
        cost_estimate=pl.CostEstimate(
            flops=24 * rows * hidden * width,
            bytes_accessed=6 * hidden * width + 8 * rows * width,
            transcendentals=0,
        ),
        compiler_params=pltpu.CompilerParams(vmem_limit_bytes=VMEM_LIMIT),
    )(coef_a, coef_b, mine_a, other_a, mine_b, other_b)


def combine_kernel(match_a, match_b, ret_a, ret_b, out_ref):
    low = low_rows(match_a.shape)
    keep = low == (pl.program_id(0) == 0)
    contract_first = (((0,), (0,)), ((), ()))
    total = None
    for match, ret in ((match_a, ret_a), (match_b, ret_b)):
        chosen = jnp.where(keep, match[...], jnp.zeros_like(match))
        part = lax.dot_general(chosen, ret[...], contract_first, preferred_element_type=f32)
        total = part if total is None else total + part
    out_ref[...] = total.astype(bf16)


def combine(match_a, match_b, ret_a, ret_b):
    rows, count = match_a.shape
    half = ret_a.shape[1]
    block = half // 2
    whole = lambda h, i: (0, 0)
    return pl.pallas_call(
        combine_kernel,
        grid=(2, half // block),
        in_specs=[pl.BlockSpec((rows, count), whole)] * 2
        + [pl.BlockSpec((rows, block), lambda h, i: (0, i))] * 2,
        out_specs=pl.BlockSpec((count, block), lambda h, i: (0, h * (half // block) + i)),
        out_shape=jax.ShapeDtypeStruct((count, 2 * half), bf16),
        name="combine",
        cost_estimate=pl.CostEstimate(
            flops=8 * rows * count * half, bytes_accessed=8 * rows * half, transcendentals=0
        ),
        compiler_params=pltpu.CompilerParams(vmem_limit_bytes=VMEM_LIMIT),
    )(match_a, match_b, ret_a, ret_b)


def exchange(rows, experts):
    blocks = rows.reshape(experts, CAP, rows.shape[1])
    return lax.all_to_all(blocks, "ep", split_axis=0, concat_axis=0, tiled=True).reshape(rows.shape)


def swap(value):
    return lax.ppermute(value, "tp", [(0, 1), (1, 0)])


def local(tokens, expert_ids, gate_weights, grad_out, w_gate, w_up, w_down):
    experts = lax.axis_size("ep")
    ids, gates = expert_ids.T, gate_weights.T
    weights = (w_gate[0], w_up[0], w_down[0])
    match, mine, other, coef, ret = [], [], [], [], []
    for chunk in range(2):
        send, found = gather(chunk, experts, ids, gates, tokens, grad_out)
        match.append(found)
        mine.append(exchange(send, experts))
    for chunk in range(2):
        other.append(swap(mine[chunk]))
        own, partner, terms = expert_terms(mine[chunk], other[chunk], *weights)
        coef.append(terms)
        summed = (own + swap(partner).astype(f32)).astype(bf16)
        ret.append(exchange(summed, experts))
    grads = weight_grads(coef[0], coef[1], mine[0], other[0], mine[1], other[1])
    grad_tokens = combine(match[0], match[1], ret[0], ret[1])
    return (grad_tokens, *(g[None] for g in grads))


def solution(mesh):
    rows = P(("ep", "tp"), None)
    weight = P("ep", "tp", None)
    return jax.shard_map(
        local,
        mesh=mesh,
        in_specs=(rows, rows, rows, rows, weight, weight, weight),
        out_specs=(rows, weight, weight, weight),
        check_vma=False,
    )
```

```python
import functools

import jax
import jax.numpy as jnp
from jax import lax
from jax.experimental import pallas as pl
from jax.experimental.pallas import tpu as pltpu
from jax.sharding import PartitionSpec as P


CAP = 8
HALF = CAP // 2
VMEM_LIMIT = 65472 * 1024

f32 = jnp.float32
bf16 = jnp.bfloat16


def low_rows(shape):
    return (lax.broadcasted_iota(jnp.int32, shape, 0) & HALF) == 0


def gather_kernel(chunk, experts, ids_ref, gates_ref, tok_ref, dy_ref, send_ref, match_ref, gate_s):
    rows, count = match_ref.shape
    topk = ids_ref.shape[0]

    @pl.when(pl.program_id(0) == 0)
    def _():
        expert_at = lax.broadcasted_iota(jnp.int32, (experts, count), 0)
        member = jnp.zeros((experts, count), f32)
        for k in range(topk):
            member += jnp.where(ids_ref[k : k + 1, :] == expert_at, 1.0, 0.0)
        earlier = jnp.where(
            lax.broadcasted_iota(jnp.int32, (count, count), 0)
            < lax.broadcasted_iota(jnp.int32, (count, count), 1),
            1.0,
            0.0,
        ).astype(bf16)
        before = jnp.dot(member.astype(bf16), earlier, preferred_element_type=f32)
        row = lax.broadcasted_iota(jnp.int32, (rows, count), 0)
        wanted = row - (row & HALF) + HALF * chunk
        match = jnp.zeros((rows, count), f32)
        gate = jnp.zeros((rows, count), f32)
        for k in range(topk):
            named = ids_ref[k : k + 1, :]
            place = jnp.sum(
                jnp.where(named == expert_at, before, 0.0), axis=0, keepdims=True
            ).astype(jnp.int32)
            target = jnp.where(named < experts, named * CAP + place, -1)
            hit = target == wanted
            match = jnp.where(hit, 1.0, match)
            gate = jnp.where(hit, gates_ref[k : k + 1, :], gate)
        match_ref[...] = match.astype(bf16)
        gate_s[...] = jnp.broadcast_to(jnp.sum(gate, axis=1, keepdims=True), gate_s.shape)

    match = match_ref[...]
    picked_x = jnp.dot(match, tok_ref[...], preferred_element_type=f32)
    picked_dy = jnp.dot(match, dy_ref[...], preferred_element_type=f32)
    out = jnp.where(low_rows(picked_x.shape), picked_x, gate_s[:, :1] * picked_dy)
    send_ref[...] = out.astype(bf16)


def gather(chunk, experts, ids, gates, tokens, grad_out):
    count, width = tokens.shape
    rows = experts * CAP
    block = width // 4
    whole = lambda i: (0, 0)
    return pl.pallas_call(
        functools.partial(gather_kernel, chunk, experts),
        grid=(width // block,),
        in_specs=[
            pl.BlockSpec(ids.shape, whole),
            pl.BlockSpec(gates.shape, whole),
            pl.BlockSpec((count, block), lambda i: (0, i)),
            pl.BlockSpec((count, block), lambda i: (0, i)),
        ],
        out_specs=[
            pl.BlockSpec((rows, block), lambda i: (0, i)),
            pl.BlockSpec((rows, count), whole),
        ],
        out_shape=[
            jax.ShapeDtypeStruct((rows, width), bf16),
            jax.ShapeDtypeStruct((rows, count), bf16),
        ],
        scratch_shapes=[pltpu.VMEM((rows, 128), f32)],
        cost_estimate=pl.CostEstimate(
            flops=4 * rows * count * width, bytes_accessed=2 * width * (rows + 2 * count), transcendentals=0
        ),
        compiler_params=pltpu.CompilerParams(vmem_limit_bytes=VMEM_LIMIT),
    )(ids, gates, tokens, grad_out)


def expert_kernel(
    mine_ref, other_ref, gate_ref, up_ref, down_ref,
    own_ref, partner_ref, coef_ref,
    rows_s, joined_s, down_s, acc_s, fold_s, sems,
):
    blocks, both, block = rows_s.shape
    rows = both // 2
    hidden = down_s.shape[1]

    def copies(i):
        cols = pl.ds(pl.multiple_of(i * block, block), block)
        pairs = (
            (mine_ref.at[:, cols], rows_s.at[i, pl.ds(0, rows)]),
            (other_ref.at[:, cols], rows_s.at[i, pl.ds(rows, rows)]),
            (gate_ref.at[:, cols], joined_s.at[i, pl.ds(0, hidden)]),
            (up_ref.at[:, cols], joined_s.at[i, pl.ds(hidden, hidden)]),
            (down_ref.at[:, cols], down_s.at[i]),
        )
        return [pltpu.make_async_copy(a, b, sems.at[i, c]) for c, (a, b) in enumerate(pairs)]

    for i in range(blocks):
        for copy in copies(i):
            copy.start()

    contract_last = (((1,), (1,)), ((), ()))
    for i in range(blocks):
        for copy in copies(i):
            copy.wait()
        here = rows_s[i]
        first = lax.dot_general(here, joined_s[i], contract_last, preferred_element_type=f32)
        second = lax.dot_general(here, down_s[i], contract_last, preferred_element_type=f32)
        if i == 0:
            acc_s[:, : 2 * hidden] = first
            acc_s[:, 2 * hidden :] = second
        else:
            acc_s[:, : 2 * hidden] += first
            acc_s[:, 2 * hidden :] += second

    step = 64

    @pl.loop(0, both // step)
    def _(b):
        at = pl.ds(pl.multiple_of(b * step, step), step)
        low = low_rows((step, hidden))
        g = acc_s[at, :hidden]
        u = acc_s[at, hidden : 2 * hidden]
        a = acc_s[at, 2 * hidden :]
        g = jnp.where(low, g, pltpu.roll(g, HALF, axis=0))
        u = jnp.where(low, u, pltpu.roll(u, HALF, axis=0))
        a = jnp.where(low, pltpu.roll(a, step - HALF, axis=0), a)
        s = jax.nn.sigmoid(g)
        act = g * s * u
        d_up = a * g * s
        d_pre = a * u * s * (1.0 + g * (1.0 - s))
        zero = jnp.zeros_like(act)
        fold_s[at, :hidden] = d_pre.astype(bf16)
        fold_s[at, hidden:] = d_up.astype(bf16)
        coef_ref[at, :hidden] = jnp.where(low, d_pre, zero).astype(bf16)
        coef_ref[at, hidden : 2 * hidden] = jnp.where(low, d_up, zero).astype(bf16)
        coef_ref[at, 2 * hidden :] = jnp.where(low, zero, act).astype(bf16)

    low = low_rows((both, block))
    for i in range(blocks // 2):
        fold = fold_s[...]
        left = jnp.dot(fold, joined_s[i], preferred_element_type=f32)
        right = jnp.dot(fold, joined_s[i + blocks // 2], preferred_element_type=f32)
        out = jnp.where(low, left, right)
        own_ref[:, i * block : (i + 1) * block] = out[:rows]
        partner_ref[:, i * block : (i + 1) * block] = out[rows:].astype(bf16)


def expert_terms(mine, other, w_gate, w_up, w_down):
    rows, width = mine.shape
    hidden = w_gate.shape[0]
    blocks = 4
    block = width // blocks
    anywhere = pl.BlockSpec(memory_space=pl.ANY)
    hbm = pl.BlockSpec(memory_space=pl.ANY)
    vmem = pl.BlockSpec(memory_space=pltpu.VMEM)
    return pl.pallas_call(
        expert_kernel,
        in_specs=[anywhere] * 2 + [hbm] * 3,
        out_specs=[vmem] * 3,
        out_shape=[
            jax.ShapeDtypeStruct((rows, width // 2), f32),
            jax.ShapeDtypeStruct((rows, width // 2), bf16),
            jax.ShapeDtypeStruct((2 * rows, 3 * hidden), bf16),
        ],
        scratch_shapes=[
            pltpu.VMEM((blocks, 2 * rows, block), bf16),
            pltpu.VMEM((blocks, 2 * hidden, block), bf16),
            pltpu.VMEM((blocks, hidden, block), bf16),
            pltpu.VMEM((2 * rows, 3 * hidden), f32),
            pltpu.VMEM((2 * rows, 2 * hidden), bf16),
            pltpu.SemaphoreType.DMA((blocks, 5)),
        ],
        name="expert_terms",
        cost_estimate=pl.CostEstimate(
            flops=20 * rows * hidden * width,
            bytes_accessed=6 * hidden * width + 7 * rows * width,
            transcendentals=2 * rows * hidden,
        ),
        compiler_params=pltpu.CompilerParams(vmem_limit_bytes=VMEM_LIMIT),
    )(mine, other, w_gate, w_up, w_down)


def weight_kernel(coef_a, coef_b, mine_a, other_a, mine_b, other_b, gate_ref, up_ref, down_ref, turned):
    both = coef_a.shape[0]
    hidden = gate_ref.shape[0]

    @pl.when(pl.program_id(0) == 0)
    def _():
        turned[:, :both] = coef_a[...].T
        turned[:, both:] = coef_b[...].T

    rows = jnp.concatenate([mine_a[...], other_a[...], mine_b[...], other_b[...]], axis=0)
    for k, out in enumerate((gate_ref, up_ref, down_ref)):
        out[...] = jnp.dot(
            turned[k * hidden : (k + 1) * hidden, :], rows, preferred_element_type=f32
        ).astype(bf16)


def weight_grads(coef_a, coef_b, mine_a, other_a, mine_b, other_b):
    rows, width = mine_a.shape
    hidden = coef_a.shape[1] // 3
    block = 512
    whole = lambda i: (0, 0)
    cols = lambda i: (0, i)
    return pl.pallas_call(
        weight_kernel,
        grid=(width // block,),
        in_specs=[pl.BlockSpec(coef_a.shape, whole)] * 2 + [pl.BlockSpec((rows, block), cols)] * 4,
        out_specs=[pl.BlockSpec((hidden, block), cols)] * 3,
        out_shape=[jax.ShapeDtypeStruct((hidden, width), bf16)] * 3,
        scratch_shapes=[pltpu.VMEM((3 * hidden, 4 * rows), bf16)],
        name="weight_grads",
        cost_estimate=pl.CostEstimate(
            flops=24 * rows * hidden * width,
            bytes_accessed=6 * hidden * width + 8 * rows * width,
            transcendentals=0,
        ),
        compiler_params=pltpu.CompilerParams(vmem_limit_bytes=VMEM_LIMIT),
    )(coef_a, coef_b, mine_a, other_a, mine_b, other_b)


def combine_kernel(match_a, match_b, ret_a, ret_b, out_ref):
    low = low_rows(match_a.shape)
    keep = low == (pl.program_id(0) == 0)
    contract_first = (((0,), (0,)), ((), ()))
    total = None
    for match, ret in ((match_a, ret_a), (match_b, ret_b)):
        chosen = jnp.where(keep, match[...], jnp.zeros_like(match))
        part = lax.dot_general(chosen, ret[...], contract_first, preferred_element_type=f32)
        total = part if total is None else total + part
    out_ref[...] = total.astype(bf16)


def combine(match_a, match_b, ret_a, ret_b):
    rows, count = match_a.shape
    half = ret_a.shape[1]
    block = half // 2
    whole = lambda h, i: (0, 0)
    return pl.pallas_call(
        combine_kernel,
        grid=(2, half // block),
        in_specs=[pl.BlockSpec((rows, count), whole)] * 2
        + [pl.BlockSpec((rows, block), lambda h, i: (0, i))] * 2,
        out_specs=pl.BlockSpec((count, block), lambda h, i: (0, h * (half // block) + i)),
        out_shape=jax.ShapeDtypeStruct((count, 2 * half), bf16),
        name="combine",
        cost_estimate=pl.CostEstimate(
            flops=8 * rows * count * half, bytes_accessed=4 * (rows + count) * half, transcendentals=0
        ),
        compiler_params=pltpu.CompilerParams(vmem_limit_bytes=VMEM_LIMIT),
    )(match_a, match_b, ret_a, ret_b)


def exchange(rows):
    return lax.all_to_all(rows, "ep", split_axis=0, concat_axis=0, tiled=True)


def swap(value):
    return lax.ppermute(value, "tp", [(0, 1), (1, 0)])


def local(tokens, expert_ids, gate_weights, grad_out, w_gate, w_up, w_down):
    experts = lax.axis_size("ep")
    ids, gates = expert_ids.T, gate_weights.T
    weights = (w_gate[0], w_up[0], w_down[0])
    match, mine, other, coef, ret = [], [], [], [], []
    for chunk in range(2):
        send, found = gather(chunk, experts, ids, gates, tokens, grad_out)
        match.append(found)
        mine.append(exchange(send))
    for chunk in range(2):
        other.append(swap(mine[chunk]))
        own, partner, terms = expert_terms(mine[chunk], other[chunk], *weights)
        coef.append(terms)
        theirs = swap(partner)
        summed = (own + theirs.astype(f32)).astype(bf16)
        ret.append(exchange(summed))
    grads = weight_grads(coef[0], coef[1], mine[0], other[0], mine[1], other[1])
    grad_tokens = combine(match[0], match[1], ret[0], ret[1])
    return (grad_tokens, *(g[None] for g in grads))


def solution(mesh):
    rows = P(("ep", "tp"), None)
    weight = P("ep", "tp", None)
    return jax.shard_map(
        local,
        mesh=mesh,
        in_specs=(rows, rows, rows, rows, weight, weight, weight),
        out_specs=(rows, weight, weight, weight),
        check_vma=False,
    )
```

```python
import functools

import jax
import jax.numpy as jnp
from jax import lax
from jax.experimental import pallas as pl
from jax.experimental.pallas import tpu as pltpu
from jax.sharding import PartitionSpec as P


CAP = 8
MIB = 1 << 20

f32 = jnp.float32
bf16 = jnp.bfloat16


def in_hbm(x):
    return pltpu.with_memory_space_constraint(x, pltpu.HBM)


def in_vmem(x):
    return pltpu.with_memory_space_constraint(x, pltpu.VMEM)


def route(experts, ids_ref, gates_ref, match_ref, gate_s):
    rows, count = match_ref.shape
    expert_at = lax.broadcasted_iota(jnp.int32, (experts, count), 0)
    member = jnp.zeros((experts, count), f32)
    for k in range(ids_ref.shape[0]):
        member += jnp.where(ids_ref[k : k + 1, :] == expert_at, 1.0, 0.0)
    earlier = jnp.where(
        lax.broadcasted_iota(jnp.int32, (count, count), 0)
        < lax.broadcasted_iota(jnp.int32, (count, count), 1),
        1.0,
        0.0,
    ).astype(bf16)
    before = jnp.dot(member.astype(bf16), earlier, preferred_element_type=f32)
    row = lax.broadcasted_iota(jnp.int32, (rows, count), 0)
    match = jnp.zeros((rows, count), f32)
    gate = jnp.zeros((rows, count), f32)
    for k in range(ids_ref.shape[0]):
        named = ids_ref[k : k + 1, :]
        place = jnp.sum(
            jnp.where(named == expert_at, before, 0.0), axis=0, keepdims=True
        ).astype(jnp.int32)
        hit = jnp.where(named < experts, named * CAP + place, -1) == row
        match = jnp.where(hit, 1.0, match)
        gate = jnp.where(hit, gates_ref[k : k + 1, :], gate)
    match_ref[...] = match.astype(bf16)
    gate_s[...] = jnp.broadcast_to(jnp.sum(gate, axis=1, keepdims=True), gate_s.shape)


def gather_kernel(experts, half, ids_ref, gates_ref, tok_ref, dy_ref, send_ref, match_ref, gate_s):
    step = pl.program_id(0)

    @pl.when(step == 0)
    def _():
        route(experts, ids_ref, gates_ref, match_ref, gate_s)

    @pl.when(step < half)
    def _():
        send_ref[...] = jnp.dot(
            match_ref[...], tok_ref[...], preferred_element_type=f32
        ).astype(bf16)

    @pl.when(step >= half)
    def _():
        picked = jnp.dot(match_ref[...], dy_ref[...], preferred_element_type=f32)
        send_ref[...] = (gate_s[:, :1] * picked).astype(bf16)


def gather(experts, ids, gates, tokens, grad_out):
    count, width = tokens.shape
    rows = experts * CAP
    half = 2
    block = width // half
    whole = lambda i: (0, 0)
    return pl.pallas_call(
        functools.partial(gather_kernel, experts, half),
        grid=(2 * half,),
        in_specs=[
            pl.BlockSpec(ids.shape, whole),
            pl.BlockSpec(gates.shape, whole),
            pl.BlockSpec((count, block), lambda i: (0, jnp.minimum(i, half - 1))),
            pl.BlockSpec((count, block), lambda i: (0, jnp.maximum(i - half, 0))),
        ],
        out_specs=[
            pl.BlockSpec((rows, block), lambda i: (0, i)),
            pl.BlockSpec((rows, count), whole),
        ],
        out_shape=[
            pltpu.HBM((rows, 2 * width), bf16),
            jax.ShapeDtypeStruct((rows, count), bf16),
        ],
        scratch_shapes=[pltpu.VMEM((rows, 128), f32)],
        name="gather",
        cost_estimate=pl.CostEstimate(
            flops=4 * rows * count * width, bytes_accessed=4 * width * (rows + count), transcendentals=0
        ),
        compiler_params=pltpu.CompilerParams(vmem_limit_bytes=12 * MIB + 16 * rows * block),
    )(in_hbm(ids), in_hbm(gates), in_hbm(tokens), in_hbm(grad_out))


def expert_kernel(
    recv_ref, gate_a, up_a, down_a, gate_b, up_b, down_b, ret_ref, own_ref, partner_ref,
    joined_s, down_s, acc_s, out_s, sems, out_sems,
):
    chunks, chunk = down_s.shape[:2]
    width = acc_s.shape[1]
    hidden = gate_a.shape[0]
    half = chunks // 2

    def load(c, refs):
        at = pl.ds((c % half) * chunk, chunk)
        dsts = (joined_s.at[c, pl.ds(0, chunk)], joined_s.at[c, pl.ds(chunk, chunk)], down_s.at[c])
        return [
            pltpu.make_async_copy(ref.at[at], dst, sems.at[c, k])
            for k, (ref, dst) in enumerate(zip(refs, dsts))
        ]

    own, partner = (gate_a, up_a, down_a), (gate_b, up_b, down_b)
    for c in range(chunks):
        for copy in load(c, own if c < half else partner):
            copy.start()

    contract_last = (((1,), (1,)), ((), ()))
    blocks = out_s.shape[0]
    block = width // blocks
    for h, coef_ref in enumerate((own_ref, partner_ref)):

        @pl.loop(0, half)
        def _(b):
            c = h * half + b
            for k, dst in enumerate(
                (joined_s.at[c, pl.ds(0, chunk)], joined_s.at[c, pl.ds(chunk, chunk)], down_s.at[c])
            ):
                pltpu.make_async_copy(gate_a.at[pl.ds(0, chunk)], dst, sems.at[c, k]).wait()
            both = lax.dot_general(
                recv_ref[:, :width], joined_s[c], contract_last, preferred_element_type=f32
            )
            a = lax.dot_general(
                recv_ref[:, width:], down_s[c], contract_last, preferred_element_type=f32
            )
            g, u = both[:, :chunk], both[:, chunk:]
            s = jax.nn.sigmoid(g)
            d_pre = (a * u * s * (1.0 + g * (1.0 - s))).astype(bf16)
            d_up = (a * g * s).astype(bf16)
            at = b * chunk
            coef_ref[:, pl.ds(pl.multiple_of(at, chunk), chunk)] = d_pre
            coef_ref[:, pl.ds(pl.multiple_of(hidden + at, chunk), chunk)] = d_up
            coef_ref[:, pl.ds(pl.multiple_of(2 * hidden + at, chunk), chunk)] = (g * s * u).astype(bf16)
            fold = jnp.concatenate([d_pre, d_up], axis=1)
            for i in range(blocks):
                cols = slice(i * block, (i + 1) * block)
                part = jnp.dot(fold, joined_s[c, :, cols], preferred_element_type=f32)
                if h:
                    acc_s[:, cols] += part
                    continue

                @pl.when(b == 0)
                def _():
                    acc_s[:, cols] = part

                @pl.when(b > 0)
                def _():
                    acc_s[:, cols] += part

    def store(i):
        return pltpu.make_async_copy(
            out_s.at[i], ret_ref.at[:, pl.ds(i * block, block)], out_sems.at[i]
        )

    for i in range(blocks):
        out_s[i] = acc_s[:, i * block : (i + 1) * block].astype(bf16)
        store(i).start()
    for i in range(blocks):
        store(i).wait()


def expert_terms(recv, own, partner):
    rows, width = recv.shape[0], recv.shape[1] // 2
    hidden = own[0].shape[0]
    chunk = 128
    chunks = 2 * hidden // chunk
    blocks = 4
    anywhere = pl.BlockSpec(memory_space=pl.ANY)
    vmem = pl.BlockSpec(memory_space=pltpu.VMEM)
    coef = jax.ShapeDtypeStruct((rows, 3 * hidden), bf16)
    return pl.pallas_call(
        expert_kernel,
        in_specs=[vmem] + [anywhere] * 6,
        out_specs=[anywhere, vmem, vmem],
        out_shape=[pltpu.HBM((rows, width), bf16), coef, coef],
        scratch_shapes=[
            pltpu.VMEM((chunks, 2 * chunk, width), bf16),
            pltpu.VMEM((chunks, chunk, width), bf16),
            pltpu.VMEM((rows, width), f32),
            pltpu.VMEM((blocks, rows, width // blocks), bf16),
            pltpu.SemaphoreType.DMA((chunks, 3)),
            pltpu.SemaphoreType.DMA((blocks,)),
        ],
        name="expert_terms",
        cost_estimate=pl.CostEstimate(
            flops=20 * rows * hidden * width,
            bytes_accessed=12 * hidden * width + 6 * rows * width,
            transcendentals=2 * rows * hidden,
        ),
        compiler_params=pltpu.CompilerParams(
            vmem_limit_bytes=8 * MIB + 12 * hidden * width + 8 * rows * width
        ),
    )(in_vmem(recv), *(in_hbm(w) for w in (*own, *partner)))


def weight_kernel(coef_a, coef_b, x_a, dy_a, x_b, dy_b, gate_ref, up_ref, down_ref, turned):
    rows = coef_a.shape[0]
    hidden = gate_ref.shape[0]

    @pl.when(pl.program_id(0) == 0)
    def _():
        turned[:, :rows] = coef_a[...].T
        turned[:, rows:] = coef_b[...].T

    x = jnp.concatenate([x_a[...], x_b[...]], axis=0)
    dy = jnp.concatenate([dy_a[...], dy_b[...]], axis=0)
    for k, (out, right) in enumerate(((gate_ref, x), (up_ref, x), (down_ref, dy))):
        out[...] = jnp.dot(
            turned[k * hidden : (k + 1) * hidden, :], right, preferred_element_type=f32
        ).astype(bf16)


def weight_grads(coef_a, coef_b, rows_a, rows_b):
    rows, width = rows_a.shape[0], rows_a.shape[1] // 2
    hidden = coef_a.shape[1] // 3
    block = 512
    blocks = width // block
    whole = lambda i: (0, 0)
    x_at = pl.BlockSpec((rows, block), lambda i: (0, i))
    dy_at = pl.BlockSpec((rows, block), lambda i: (0, blocks + i))
    rows_a, rows_b = in_hbm(rows_a), in_hbm(rows_b)
    return pl.pallas_call(
        weight_kernel,
        grid=(blocks,),
        in_specs=[pl.BlockSpec(coef_a.shape, whole)] * 2 + [x_at, dy_at] * 2,
        out_specs=[pl.BlockSpec((hidden, block), lambda i: (0, i))] * 3,
        out_shape=[jax.ShapeDtypeStruct((hidden, width), bf16)] * 3,
        scratch_shapes=[pltpu.VMEM((3 * hidden, 2 * rows), bf16)],
        name="weight_grads",
        cost_estimate=pl.CostEstimate(
            flops=12 * rows * hidden * width,
            bytes_accessed=6 * hidden * width + 8 * rows * width,
            transcendentals=0,
        ),
        compiler_params=pltpu.CompilerParams(vmem_limit_bytes=65472 * 1024),
    )(coef_a, coef_b, rows_a, rows_a, rows_b, rows_b)


def combine_kernel(turned_ref, ret_ref, out_ref):
    out_ref[...] = jnp.dot(
        turned_ref[...], ret_ref[...], preferred_element_type=f32
    ).astype(bf16)


def combine(turned, ret):
    count, rows = turned.shape
    width = ret.shape[1]
    block = width // 4
    return pl.pallas_call(
        combine_kernel,
        grid=(width // block,),
        in_specs=[
            pl.BlockSpec((count, rows), lambda i: (0, 0)),
            pl.BlockSpec((rows, block), lambda i: (0, i)),
        ],
        out_specs=pl.BlockSpec((count, block), lambda i: (0, i)),
        out_shape=jax.ShapeDtypeStruct((count, width), bf16),
        name="combine",
        cost_estimate=pl.CostEstimate(
            flops=2 * rows * count * width, bytes_accessed=2 * (rows + count) * width, transcendentals=0
        ),
        compiler_params=pltpu.CompilerParams(vmem_limit_bytes=65472 * 1024),
    )(turned, ret)


def exchange(rows):
    return lax.all_to_all(rows, "ep", split_axis=0, concat_axis=0, tiled=True)


def swap(value):
    return lax.ppermute(value, "tp", [(0, 1), (1, 0)])


def local(tokens, expert_ids, gate_weights, grad_out, w_gate, w_up, w_down):
    experts = lax.axis_size("ep")
    own = (w_gate[0], w_up[0], w_down[0])
    send, match = gather(experts, expert_ids.T, gate_weights.T, tokens, grad_out)
    recv = exchange(send)
    partner = tuple(swap(w) for w in own)
    turned = match.T
    ret, coef, coef_sent = expert_terms(recv, own, partner)
    back = exchange(ret)
    coef_got, rows_got = swap(coef_sent), swap(recv)
    grads = weight_grads(coef, coef_got, recv, rows_got)
    grad_tokens = combine(turned, back)
    return (grad_tokens, *(g[None] for g in grads))


def solution(mesh):
    rows = P(("ep", "tp"), None)
    weight = P("ep", "tp", None)
    return jax.shard_map(
        local,
        mesh=mesh,
        in_specs=(rows, rows, rows, rows, weight, weight, weight),
        out_specs=(rows, weight, weight, weight),
        check_vma=False,
    )
```

```python
import functools

import jax
import jax.numpy as jnp
from jax import lax
from jax.experimental import pallas as pl
from jax.experimental.pallas import tpu as pltpu
from jax.sharding import PartitionSpec as P


CAP = 8
MIB = 1 << 20

f32 = jnp.float32
bf16 = jnp.bfloat16


def in_hbm(x):
    return pltpu.with_memory_space_constraint(x, pltpu.HBM)


def in_vmem(x):
    return pltpu.with_memory_space_constraint(x, pltpu.VMEM)


def route(experts, ids_ref, gates_ref, match_ref, gate_s):
    rows, count = match_ref.shape
    expert_at = lax.broadcasted_iota(jnp.int32, (experts, count), 0)
    member = jnp.zeros((experts, count), f32)
    for k in range(ids_ref.shape[0]):
        member += jnp.where(ids_ref[k : k + 1, :] == expert_at, 1.0, 0.0)
    earlier = jnp.where(
        lax.broadcasted_iota(jnp.int32, (count, count), 0)
        < lax.broadcasted_iota(jnp.int32, (count, count), 1),
        1.0,
        0.0,
    ).astype(bf16)
    before = jnp.dot(member.astype(bf16), earlier, preferred_element_type=f32)
    row = lax.broadcasted_iota(jnp.int32, (rows, count), 0)
    match = jnp.zeros((rows, count), f32)
    gate = jnp.zeros((rows, count), f32)
    for k in range(ids_ref.shape[0]):
        named = ids_ref[k : k + 1, :]
        place = jnp.sum(
            jnp.where(named == expert_at, before, 0.0), axis=0, keepdims=True
        ).astype(jnp.int32)
        hit = jnp.where(named < experts, named * CAP + place, -1) == row
        match = jnp.where(hit, 1.0, match)
        gate = jnp.where(hit, gates_ref[k : k + 1, :], gate)
    match_ref[...] = match.astype(bf16)
    gate_s[...] = jnp.broadcast_to(jnp.sum(gate, axis=1, keepdims=True), gate_s.shape)


def gather_kernel(
    experts, ids_ref, gates_ref, tok_ref, dy_ref, send_ref, match_ref,
    ids_s, gates_s, rows_s, match_s, gate_s, out_s, sems, out_sems,
):
    blocks, _, block = rows_s.shape
    half = blocks // 2
    small = [
        pltpu.make_async_copy(ids_ref, ids_s, sems.at[blocks]),
        pltpu.make_async_copy(gates_ref, gates_s, sems.at[blocks + 1]),
    ]

    def load(i):
        src = tok_ref if i < half else dy_ref
        cols = pl.ds(i % half * block, block)
        return pltpu.make_async_copy(src.at[:, cols], rows_s.at[i], sems.at[i])

    def store(i):
        cols = pl.ds(i * block, block)
        return pltpu.make_async_copy(out_s.at[i], send_ref.at[:, cols], out_sems.at[i])

    for copy in small:
        copy.start()
    for i in range(blocks):
        load(i).start()
    for copy in small:
        copy.wait()
    route(experts, ids_s, gates_s, match_s, gate_s)
    keep = pltpu.make_async_copy(match_s, match_ref, out_sems.at[blocks])
    for i in range(blocks):
        load(i).wait()
        picked = jnp.dot(match_s[...], rows_s[i], preferred_element_type=f32)
        if i >= half:
            picked = gate_s[:, :1] * picked
        out_s[i] = picked.astype(bf16)
        store(i).start()
    keep.start()
    for i in range(blocks):
        store(i).wait()
    keep.wait()


def gather(experts, ids, gates, tokens, grad_out):
    count, width = tokens.shape
    rows = experts * CAP
    blocks = 8
    block = 2 * width // blocks
    anywhere = pl.BlockSpec(memory_space=pl.ANY)
    return pl.pallas_call(
        functools.partial(gather_kernel, experts),
        in_specs=[anywhere] * 4,
        out_specs=[anywhere] * 2,
        out_shape=[pltpu.HBM((rows, 2 * width), bf16), pltpu.HBM((rows, count), bf16)],
        scratch_shapes=[
            pltpu.VMEM(ids.shape, ids.dtype),
            pltpu.VMEM(gates.shape, gates.dtype),
            pltpu.VMEM((blocks, count, block), bf16),
            pltpu.VMEM((rows, count), bf16),
            pltpu.VMEM((rows, 128), f32),
            pltpu.VMEM((blocks, rows, block), bf16),
            pltpu.SemaphoreType.DMA((blocks + 2,)),
            pltpu.SemaphoreType.DMA((blocks + 1,)),
        ],
        name="gather",
        cost_estimate=pl.CostEstimate(
            flops=4 * rows * count * width, bytes_accessed=4 * width * (rows + count), transcendentals=0
        ),
        compiler_params=pltpu.CompilerParams(
            vmem_limit_bytes=8 * MIB + 8 * width * (rows + count)
        ),
    )(in_hbm(ids), in_hbm(gates), in_hbm(tokens), in_hbm(grad_out))


def expert_kernel(
    recv_ref, gate_a, up_a, down_a, gate_b, up_b, down_b, ret_ref, own_ref, partner_ref,
    joined_s, down_s, pre_s, dact_s, fold_s, total_s, coef_s, out_s, sems, coef_sems, out_sems,
):
    blocks, _, block = joined_s.shape
    hidden = gate_a.shape[0]
    width = blocks * block
    halves = ((gate_a, up_a, down_a), (gate_b, up_b, down_b))

    def loads(h, i):
        cols = pl.ds(i * block, block)
        dsts = (
            joined_s.at[i, pl.ds(2 * h * hidden, hidden)],
            joined_s.at[i, pl.ds((2 * h + 1) * hidden, hidden)],
            down_s.at[i, pl.ds(h * hidden, hidden)],
        )
        return [
            pltpu.make_async_copy(ref.at[:, cols], dst, sems.at[h, i, k])
            for k, (ref, dst) in enumerate(zip(halves[h], dsts))
        ]

    def store(i):
        return pltpu.make_async_copy(
            out_s.at[i], ret_ref.at[:, pl.ds(i * block, block)], out_sems.at[i]
        )

    for h in range(2):
        for i in range(blocks):
            for copy in loads(h, i):
                copy.start()

    contract_last = (((1,), (1,)), ((), ()))
    kept = []
    for h, coef_ref in enumerate((own_ref, partner_ref)):
        for i in range(blocks):
            for copy in loads(h, i):
                copy.wait()
            x = recv_ref[:, i * block : (i + 1) * block]
            dy = recv_ref[:, width + i * block : width + (i + 1) * block]
            pre = lax.dot_general(
                joined_s[i, 2 * h * hidden : 2 * (h + 1) * hidden],
                x,
                contract_last,
                preferred_element_type=f32,
            )
            dact = lax.dot_general(
                down_s[i, h * hidden : (h + 1) * hidden],
                dy,
                contract_last,
                preferred_element_type=f32,
            )
            pre_s[...] = pre if i == 0 else pre_s[...] + pre
            dact_s[...] = dact if i == 0 else dact_s[...] + dact

        step = 32

        @pl.loop(0, hidden // step)
        def _(b):
            at = pl.multiple_of(b * step, step)
            g = pre_s[pl.ds(at, step), :]
            u = pre_s[pl.ds(hidden + at, step), :]
            a = dact_s[pl.ds(at, step), :]
            s = jax.nn.sigmoid(g)
            d_pre = (a * u * s * (1.0 + g * (1.0 - s))).astype(bf16)
            d_up = (a * g * s).astype(bf16)
            coef_s[h, pl.ds(at, step), :] = d_pre
            coef_s[h, pl.ds(hidden + at, step), :] = d_up
            coef_s[h, pl.ds(2 * hidden + at, step), :] = (g * s * u).astype(bf16)

        kept.append(pltpu.make_async_copy(coef_s.at[h], coef_ref, coef_sems.at[h]))
        kept[h].start()
        fold_s[...] = coef_s[h, : 2 * hidden, :].T
        for i in range(blocks):
            part = jnp.dot(
                fold_s[...],
                joined_s[i, 2 * h * hidden : 2 * (h + 1) * hidden],
                preferred_element_type=f32,
            )
            if h == 0:
                total_s[i] = part
            else:
                out_s[i] = (total_s[i] + part).astype(bf16)
                store(i).start()
    for i in range(blocks):
        store(i).wait()
    for copy in kept:
        copy.wait()


def expert_terms(recv, own, partner):
    rows, width = recv.shape[0], recv.shape[1] // 2
    hidden = own[0].shape[0]
    blocks = 4
    block = width // blocks
    anywhere = pl.BlockSpec(memory_space=pl.ANY)
    vmem = pl.BlockSpec(memory_space=pltpu.VMEM)
    coef = pltpu.HBM((3 * hidden, rows), bf16)
    return pl.pallas_call(
        expert_kernel,
        in_specs=[vmem] + [anywhere] * 6,
        out_specs=[anywhere] * 3,
        out_shape=[pltpu.HBM((rows, width), bf16), coef, coef],
        scratch_shapes=[
            pltpu.VMEM((blocks, 4 * hidden, block), bf16),
            pltpu.VMEM((blocks, 2 * hidden, block), bf16),
            pltpu.VMEM((2 * hidden, rows), f32),
            pltpu.VMEM((hidden, rows), f32),
            pltpu.VMEM((rows, 2 * hidden), bf16),
            pltpu.VMEM((blocks, rows, block), f32),
            pltpu.VMEM((2, 3 * hidden, rows), bf16),
            pltpu.VMEM((blocks, rows, block), bf16),
            pltpu.SemaphoreType.DMA((2, blocks, 3)),
            pltpu.SemaphoreType.DMA((2,)),
            pltpu.SemaphoreType.DMA((blocks,)),
        ],
        name="expert_terms",
        cost_estimate=pl.CostEstimate(
            flops=20 * rows * hidden * width,
            bytes_accessed=12 * hidden * width + 6 * rows * width,
            transcendentals=2 * rows * hidden,
        ),
        compiler_params=pltpu.CompilerParams(
            vmem_limit_bytes=8 * MIB + 12 * hidden * width + 8 * rows * width + 40 * rows * hidden
        ),
    )(in_vmem(recv), *(in_hbm(w) for w in (*own, *partner)))


def weight_kernel(coef_a, coef_b, x_a, dy_a, x_b, dy_b, gate_ref, up_ref, down_ref):
    hidden = gate_ref.shape[0]
    x = jnp.concatenate([x_a[...], x_b[...]], axis=0)
    dy = jnp.concatenate([dy_a[...], dy_b[...]], axis=0)
    for k, (out, right) in enumerate(((gate_ref, x), (up_ref, x), (down_ref, dy))):
        at = slice(k * hidden, (k + 1) * hidden)
        left = jnp.concatenate([coef_a[at, :], coef_b[at, :]], axis=1)
        out[...] = jnp.dot(left, right, preferred_element_type=f32).astype(bf16)


def weight_grads(coef_a, coef_b, rows_a, rows_b):
    rows, width = rows_a.shape[0], rows_a.shape[1] // 2
    hidden = coef_a.shape[0] // 3
    block = 512
    blocks = width // block
    whole = lambda i: (0, 0)
    x_at = pl.BlockSpec((rows, block), lambda i: (0, i))
    dy_at = pl.BlockSpec((rows, block), lambda i: (0, blocks + i))
    rows_a, rows_b = in_hbm(rows_a), in_hbm(rows_b)
    return pl.pallas_call(
        weight_kernel,
        grid=(blocks,),
        in_specs=[pl.BlockSpec(coef_a.shape, whole)] * 2 + [x_at, dy_at] * 2,
        out_specs=[pl.BlockSpec((hidden, block), lambda i: (0, i))] * 3,
        out_shape=[jax.ShapeDtypeStruct((hidden, width), bf16)] * 3,
        name="weight_grads",
        cost_estimate=pl.CostEstimate(
            flops=12 * rows * hidden * width,
            bytes_accessed=6 * hidden * width + 8 * rows * width,
            transcendentals=0,
        ),
        compiler_params=pltpu.CompilerParams(vmem_limit_bytes=65472 * 1024),
    )(in_hbm(coef_a), in_hbm(coef_b), rows_a, rows_a, rows_b, rows_b)


def combine_kernel(turned_ref, ret_ref, out_ref, turned_s, ret_s, out_s, sems, out_sems):
    blocks, _, block = ret_s.shape

    def load(i):
        cols = pl.ds(i * block, block)
        return pltpu.make_async_copy(ret_ref.at[:, cols], ret_s.at[i], sems.at[i])

    def store(i):
        cols = pl.ds(i * block, block)
        return pltpu.make_async_copy(out_s.at[i], out_ref.at[:, cols], out_sems.at[i])

    first = pltpu.make_async_copy(turned_ref, turned_s, sems.at[blocks])
    first.start()
    for i in range(blocks):
        load(i).start()
    first.wait()
    for i in range(blocks):
        load(i).wait()
        out_s[i] = jnp.dot(turned_s[...], ret_s[i], preferred_element_type=f32).astype(bf16)
        store(i).start()
    for i in range(blocks):
        store(i).wait()


def combine(turned, ret):
    count, rows = turned.shape
    width = ret.shape[1]
    blocks = 4
    block = width // blocks
    anywhere = pl.BlockSpec(memory_space=pl.ANY)
    return pl.pallas_call(
        combine_kernel,
        in_specs=[anywhere] * 2,
        out_specs=anywhere,
        out_shape=pltpu.HBM((count, width), bf16),
        scratch_shapes=[
            pltpu.VMEM((count, rows), bf16),
            pltpu.VMEM((blocks, rows, block), bf16),
            pltpu.VMEM((blocks, count, block), bf16),
            pltpu.SemaphoreType.DMA((blocks + 1,)),
            pltpu.SemaphoreType.DMA((blocks,)),
        ],
        name="combine",
        cost_estimate=pl.CostEstimate(
            flops=2 * rows * count * width, bytes_accessed=2 * (rows + count) * width, transcendentals=0
        ),
        compiler_params=pltpu.CompilerParams(
            vmem_limit_bytes=8 * MIB + 4 * (rows + count) * width
        ),
    )(in_hbm(turned), in_hbm(ret))


def exchange(rows):
    return lax.all_to_all(rows, "ep", split_axis=0, concat_axis=0, tiled=True)


def swap(value):
    return lax.ppermute(value, "tp", [(0, 1), (1, 0)])


def local(tokens, expert_ids, gate_weights, grad_out, w_gate, w_up, w_down):
    experts = lax.axis_size("ep")
    own = (w_gate[0], w_up[0], w_down[0])
    send, match = gather(experts, expert_ids.T, gate_weights.T, tokens, grad_out)
    recv = exchange(send)
    partner = tuple(swap(w) for w in own)
    turned = match.T
    ret, coef, coef_sent = expert_terms(recv, own, partner)
    back = exchange(ret)
    coef_got, rows_got = swap(coef_sent), swap(recv)
    grads = weight_grads(coef, coef_got, recv, rows_got)
    grad_tokens = combine(turned, back)
    return (grad_tokens, *(g[None] for g in grads))


def solution(mesh):
    rows = P(("ep", "tp"), None)
    weight = P("ep", "tp", None)
    return jax.shard_map(
        local,
        mesh=mesh,
        in_specs=(rows, rows, rows, rows, weight, weight, weight),
        out_specs=(rows, weight, weight, weight),
        check_vma=False,
    )
```

```python
import functools

import jax
import jax.numpy as jnp
from jax import lax
from jax.experimental import pallas as pl
from jax.experimental.pallas import tpu as pltpu
from jax.sharding import PartitionSpec as P


CAP = 8
MIB = 1 << 20
PIECES = 2
IN_FLIGHT = 3

f32 = jnp.float32
bf16 = jnp.bfloat16


def in_hbm(x):
    return pltpu.with_memory_space_constraint(x, pltpu.HBM)


def in_vmem(x):
    return pltpu.with_memory_space_constraint(x, pltpu.VMEM)


def route(experts, ids_ref, gates_ref, match_ref, gate_s):
    rows, count = match_ref.shape
    expert_at = lax.broadcasted_iota(jnp.int32, (experts, count), 0)
    member = jnp.zeros((experts, count), f32)
    for k in range(ids_ref.shape[0]):
        member += jnp.where(ids_ref[k : k + 1, :] == expert_at, 1.0, 0.0)
    earlier = jnp.where(
        lax.broadcasted_iota(jnp.int32, (count, count), 0)
        < lax.broadcasted_iota(jnp.int32, (count, count), 1),
        1.0,
        0.0,
    ).astype(bf16)
    before = jnp.dot(member.astype(bf16), earlier, preferred_element_type=f32)
    row = lax.broadcasted_iota(jnp.int32, (rows, count), 0)
    match = jnp.zeros((rows, count), f32)
    gate = jnp.zeros((rows, count), f32)
    for k in range(ids_ref.shape[0]):
        named = ids_ref[k : k + 1, :]
        place = jnp.sum(
            jnp.where(named == expert_at, before, 0.0), axis=0, keepdims=True
        ).astype(jnp.int32)
        hit = jnp.where(named < experts, named * CAP + place, -1) == row
        match = jnp.where(hit, 1.0, match)
        gate = jnp.where(hit, gates_ref[k : k + 1, :], gate)
    match_ref[...] = match.astype(bf16)
    gate_s[...] = jnp.broadcast_to(jnp.sum(gate, axis=1, keepdims=True), gate_s.shape)


def gather_kernel(
    experts, ids_ref, gates_ref, tok_ref, dy_ref, send_ref, match_ref,
    ids_s, gates_s, rows_s, match_s, gate_s, out_s, sems, out_sems,
):
    blocks, _, block = rows_s.shape
    half = blocks // 2
    small = [
        pltpu.make_async_copy(ids_ref, ids_s, sems.at[blocks]),
        pltpu.make_async_copy(gates_ref, gates_s, sems.at[blocks + 1]),
    ]

    def load(i):
        src = tok_ref if i < half else dy_ref
        cols = pl.ds(i % half * block, block)
        return pltpu.make_async_copy(src.at[:, cols], rows_s.at[i], sems.at[i])

    def store(i):
        cols = pl.ds(i * block, block)
        return pltpu.make_async_copy(out_s.at[i], send_ref.at[:, cols], out_sems.at[i])

    for copy in small:
        copy.start()
    for i in range(blocks):
        load(i).start()
    for copy in small:
        copy.wait()
    route(experts, ids_s, gates_s, match_s, gate_s)
    keep = pltpu.make_async_copy(match_s, match_ref, out_sems.at[blocks])
    for i in range(blocks):
        load(i).wait()
        picked = jnp.dot(match_s[...], rows_s[i], preferred_element_type=f32)
        if i >= half:
            picked = gate_s[:, :1] * picked
        out_s[i] = picked.astype(bf16)
        store(i).start()
    keep.start()
    for i in range(blocks):
        store(i).wait()
    keep.wait()


def gather(experts, ids, gates, tokens, grad_out):
    count, width = tokens.shape
    rows = experts * CAP
    blocks = 8
    block = 2 * width // blocks
    anywhere = pl.BlockSpec(memory_space=pl.ANY)
    return pl.pallas_call(
        functools.partial(gather_kernel, experts),
        in_specs=[anywhere] * 4,
        out_specs=[anywhere] * 2,
        out_shape=[pltpu.HBM((rows, 2 * width), bf16), pltpu.HBM((rows, count), bf16)],
        scratch_shapes=[
            pltpu.VMEM(ids.shape, ids.dtype),
            pltpu.VMEM(gates.shape, gates.dtype),
            pltpu.VMEM((blocks, count, block), bf16),
            pltpu.VMEM((rows, count), bf16),
            pltpu.VMEM((rows, 128), f32),
            pltpu.VMEM((blocks, rows, block), bf16),
            pltpu.SemaphoreType.DMA((blocks + 2,)),
            pltpu.SemaphoreType.DMA((blocks + 1,)),
        ],
        name="gather",
        cost_estimate=pl.CostEstimate(
            flops=4 * rows * count * width, bytes_accessed=4 * width * (rows + count), transcendentals=0
        ),
        compiler_params=pltpu.CompilerParams(
            vmem_limit_bytes=8 * MIB + 8 * width * (rows + count)
        ),
    )(in_hbm(ids), in_hbm(gates), in_hbm(tokens), in_hbm(grad_out))


def expert_kernel(
    recv_ref, gate_a, up_a, down_a, gate_b, up_b, down_b, ret_ref, own_ref, partner_ref,
    turned_s, joined_s, down_s, first_s, fold_s, total_s, coef_s, out_s, sems, coef_sems, out_sems,
):
    hidden = gate_a.shape[0]
    blocks, _, block = out_s.shape
    width = blocks * block

    size = hidden // PIECES
    units = [(h, k, p * size, size) for h in range(2) for k in range(3) for p in range(PIECES)]
    sources = ((gate_a, up_a, down_a), (gate_b, up_b, down_b))

    def held(h, k, at, size):
        if k == 2:
            return down_s.at[h, pl.ds(at, size)]
        return joined_s.at[h, pl.ds(k * hidden + at, size)]

    def load(n):
        h, k, at, size = units[n]
        return pltpu.make_async_copy(
            sources[h][k].at[pl.ds(at, size)], held(h, k, at, size), sems.at[n]
        )

    def store(i):
        return pltpu.make_async_copy(
            out_s.at[i], ret_ref.at[:, pl.ds(i * block, block)], out_sems.at[i]
        )

    for n in range(IN_FLIGHT):
        load(n).start()

    for side in range(2):
        for i in range(blocks):
            at = i * block
            turned_s[side, at : at + block, :] = recv_ref[
                :, side * width + at : side * width + at + block
            ].T
    kept = []
    for h, coef_ref in enumerate((own_ref, partner_ref)):
        for n, (half, k, at, size) in enumerate(units):
            if half != h:
                continue
            load(n).wait()
            if n + IN_FLIGHT < len(units):
                load(n + IN_FLIGHT).start()
            first_s[k * hidden + at : k * hidden + at + size, :] = jnp.dot(
                held(h, k, at, size)[...], turned_s[k // 2], preferred_element_type=f32
            )

        step = 32

        @pl.loop(0, hidden // step)
        def _(b):
            at = pl.multiple_of(b * step, step)
            g = first_s[pl.ds(at, step), :]
            u = first_s[pl.ds(hidden + at, step), :]
            a = first_s[pl.ds(2 * hidden + at, step), :]
            s = jax.nn.sigmoid(g)
            d_pre = (a * u * s * (1.0 + g * (1.0 - s))).astype(bf16)
            d_up = (a * g * s).astype(bf16)
            coef_s[h, pl.ds(at, step), :] = d_pre
            coef_s[h, pl.ds(hidden + at, step), :] = d_up
            coef_s[h, pl.ds(2 * hidden + at, step), :] = (g * s * u).astype(bf16)

        kept.append(pltpu.make_async_copy(coef_s.at[h], coef_ref, coef_sems.at[h]))
        fold_s[...] = coef_s[h, : 2 * hidden, :].T
        for i in range(blocks):
            part = jnp.dot(
                fold_s[...],
                joined_s[h, :, i * block : (i + 1) * block],
                preferred_element_type=f32,
            )
            if h == 0:
                total_s[i] = part
            else:
                out_s[i] = (total_s[i] + part).astype(bf16)
                store(i).start()
        kept[h].start()
    for i in range(blocks):
        store(i).wait()
    for copy in kept:
        copy.wait()


def expert_terms(recv, own, partner):
    rows, width = recv.shape[0], recv.shape[1] // 2
    hidden = own[0].shape[0]
    blocks = 4
    block = width // blocks
    anywhere = pl.BlockSpec(memory_space=pl.ANY)
    vmem = pl.BlockSpec(memory_space=pltpu.VMEM)
    coef = pltpu.HBM((3 * hidden, rows), bf16)
    return pl.pallas_call(
        expert_kernel,
        in_specs=[vmem] + [anywhere] * 6,
        out_specs=[anywhere] * 3,
        out_shape=[pltpu.HBM((rows, width), bf16), coef, coef],
        scratch_shapes=[
            pltpu.VMEM((2, width, rows), bf16),
            pltpu.VMEM((2, 2 * hidden, width), bf16),
            pltpu.VMEM((2, hidden, width), bf16),
            pltpu.VMEM((3 * hidden, rows), f32),
            pltpu.VMEM((rows, 2 * hidden), bf16),
            pltpu.VMEM((blocks, rows, block), f32),
            pltpu.VMEM((2, 3 * hidden, rows), bf16),
            pltpu.VMEM((blocks, rows, block), bf16),
            pltpu.SemaphoreType.DMA((6 * PIECES,)),
            pltpu.SemaphoreType.DMA((2,)),
            pltpu.SemaphoreType.DMA((blocks,)),
        ],
        name="expert_terms",
        cost_estimate=pl.CostEstimate(
            flops=20 * rows * hidden * width,
            bytes_accessed=12 * hidden * width + 6 * rows * width,
            transcendentals=2 * rows * hidden,
        ),
        compiler_params=pltpu.CompilerParams(
            vmem_limit_bytes=min(
                8 * MIB + 12 * hidden * width + 18 * rows * width, 65408 * 1024 - 4 * rows * width
            )
        ),
    )(in_vmem(recv), *(in_hbm(w) for w in (*own, *partner)))


def weight_kernel(coef_a, coef_b, x_a, dy_a, x_b, dy_b, gate_ref, up_ref, down_ref):
    hidden = gate_ref.shape[0]
    x = jnp.concatenate([x_a[...], x_b[...]], axis=0)
    dy = jnp.concatenate([dy_a[...], dy_b[...]], axis=0)
    for k, (out, right) in enumerate(((gate_ref, x), (up_ref, x), (down_ref, dy))):
        at = slice(k * hidden, (k + 1) * hidden)
        left = jnp.concatenate([coef_a[at, :], coef_b[at, :]], axis=1)
        out[...] = jnp.dot(left, right, preferred_element_type=f32).astype(bf16)


def weight_grads(coef_a, coef_b, rows_a, rows_b):
    rows, width = rows_a.shape[0], rows_a.shape[1] // 2
    hidden = coef_a.shape[0] // 3
    block = 512
    blocks = width // block
    whole = lambda i: (0, 0)
    x_at = pl.BlockSpec((rows, block), lambda i: (0, i))
    dy_at = pl.BlockSpec((rows, block), lambda i: (0, blocks + i))
    rows_a, rows_b = in_hbm(rows_a), in_hbm(rows_b)
    return pl.pallas_call(
        weight_kernel,
        grid=(blocks,),
        in_specs=[pl.BlockSpec(coef_a.shape, whole)] * 2 + [x_at, dy_at] * 2,
        out_specs=[pl.BlockSpec((hidden, block), lambda i: (0, i))] * 3,
        out_shape=[jax.ShapeDtypeStruct((hidden, width), bf16)] * 3,
        name="weight_grads",
        cost_estimate=pl.CostEstimate(
            flops=12 * rows * hidden * width,
            bytes_accessed=6 * hidden * width + 8 * rows * width,
            transcendentals=0,
        ),
        compiler_params=pltpu.CompilerParams(vmem_limit_bytes=65472 * 1024),
    )(in_hbm(coef_a), in_hbm(coef_b), rows_a, rows_a, rows_b, rows_b)


def combine_kernel(turned_ref, ret_ref, out_ref, turned_s, ret_s, out_s, sems, out_sems):
    blocks, _, block = ret_s.shape

    def load(i):
        cols = pl.ds(i * block, block)
        return pltpu.make_async_copy(ret_ref.at[:, cols], ret_s.at[i], sems.at[i])

    def store(i):
        cols = pl.ds(i * block, block)
        return pltpu.make_async_copy(out_s.at[i], out_ref.at[:, cols], out_sems.at[i])

    first = pltpu.make_async_copy(turned_ref, turned_s, sems.at[blocks])
    first.start()
    for i in range(blocks):
        load(i).start()
    first.wait()
    for i in range(blocks):
        load(i).wait()
        out_s[i] = jnp.dot(turned_s[...], ret_s[i], preferred_element_type=f32).astype(bf16)
        store(i).start()
    for i in range(blocks):
        store(i).wait()


def combine(turned, ret):
    count, rows = turned.shape
    width = ret.shape[1]
    blocks = 4
    block = width // blocks
    anywhere = pl.BlockSpec(memory_space=pl.ANY)
    return pl.pallas_call(
        combine_kernel,
        in_specs=[anywhere] * 2,
        out_specs=anywhere,
        out_shape=pltpu.HBM((count, width), bf16),
        scratch_shapes=[
            pltpu.VMEM((count, rows), bf16),
            pltpu.VMEM((blocks, rows, block), bf16),
            pltpu.VMEM((blocks, count, block), bf16),
            pltpu.SemaphoreType.DMA((blocks + 1,)),
            pltpu.SemaphoreType.DMA((blocks,)),
        ],
        name="combine",
        cost_estimate=pl.CostEstimate(
            flops=2 * rows * count * width, bytes_accessed=2 * (rows + count) * width, transcendentals=0
        ),
        compiler_params=pltpu.CompilerParams(
            vmem_limit_bytes=8 * MIB + 4 * (rows + count) * width
        ),
    )(in_hbm(turned), in_hbm(ret))


def exchange(rows):
    return lax.all_to_all(rows, "ep", split_axis=0, concat_axis=0, tiled=True)


def swap(value):
    return lax.ppermute(value, "tp", [(0, 1), (1, 0)])


def local(tokens, expert_ids, gate_weights, grad_out, w_gate, w_up, w_down):
    experts = lax.axis_size("ep")
    own = (w_gate[0], w_up[0], w_down[0])
    send, match = gather(experts, expert_ids.T, gate_weights.T, tokens, grad_out)
    recv = exchange(send)
    partner = tuple(swap(w) for w in own)
    turned = match.T
    ret, coef, coef_sent = expert_terms(recv, own, partner)
    back = exchange(ret)
    coef_got, rows_got = swap(coef_sent), swap(recv)
    grads = weight_grads(coef, coef_got, recv, rows_got)
    grad_tokens = combine(turned, back)
    return (grad_tokens, *(g[None] for g in grads))


def solution(mesh):
    rows = P(("ep", "tp"), None)
    weight = P("ep", "tp", None)
    return jax.shard_map(
        local,
        mesh=mesh,
        in_specs=(rows, rows, rows, rows, weight, weight, weight),
        out_specs=(rows, weight, weight, weight),
        check_vma=False,
    )
```

```python
import functools

import jax
import jax.numpy as jnp
from jax import lax
from jax.experimental import pallas as pl
from jax.experimental.pallas import tpu as pltpu
from jax.sharding import PartitionSpec as P


CAP = 8
MIB = 1 << 20
PIECES = 1
IN_FLIGHT = 3
PASS = 192

f32 = jnp.float32
bf16 = jnp.bfloat16


def in_hbm(x):
    return pltpu.with_memory_space_constraint(x, pltpu.HBM)


def in_vmem(x):
    return pltpu.with_memory_space_constraint(x, pltpu.VMEM)


def route(experts, ids_ref, gates_ref, match_ref, gate_s):
    rows, count = match_ref.shape
    expert_at = lax.broadcasted_iota(jnp.int32, (experts, count), 0)
    member = jnp.zeros((experts, count), f32)
    for k in range(ids_ref.shape[0]):
        member += jnp.where(ids_ref[k : k + 1, :] == expert_at, 1.0, 0.0)
    earlier = jnp.where(
        lax.broadcasted_iota(jnp.int32, (count, count), 0)
        < lax.broadcasted_iota(jnp.int32, (count, count), 1),
        1.0,
        0.0,
    ).astype(bf16)
    before = jnp.dot(member.astype(bf16), earlier, preferred_element_type=f32)
    row = lax.broadcasted_iota(jnp.int32, (rows, count), 0)
    match = jnp.zeros((rows, count), f32)
    gate = jnp.zeros((rows, count), f32)
    for k in range(ids_ref.shape[0]):
        named = ids_ref[k : k + 1, :]
        place = jnp.sum(
            jnp.where(named == expert_at, before, 0.0), axis=0, keepdims=True
        ).astype(jnp.int32)
        hit = jnp.where(named < experts, named * CAP + place, -1) == row
        match = jnp.where(hit, 1.0, match)
        gate = jnp.where(hit, gates_ref[k : k + 1, :], gate)
    match_ref[...] = match.astype(bf16)
    gate_s[...] = jnp.broadcast_to(jnp.sum(gate, axis=1, keepdims=True), gate_s.shape)


def gather_kernel(
    experts, ids_ref, gates_ref, tok_ref, dy_ref, send_ref, match_ref,
    ids_s, gates_s, rows_s, match_s, gate_s, out_s, sems, out_sems,
):
    blocks, _, block = rows_s.shape
    half = blocks // 2
    small = [
        pltpu.make_async_copy(ids_ref, ids_s, sems.at[blocks]),
        pltpu.make_async_copy(gates_ref, gates_s, sems.at[blocks + 1]),
    ]

    def load(i):
        src = tok_ref if i < half else dy_ref
        cols = pl.ds(i % half * block, block)
        return pltpu.make_async_copy(src.at[:, cols], rows_s.at[i], sems.at[i])

    def store(i):
        cols = pl.ds(i * block, block)
        return pltpu.make_async_copy(out_s.at[i], send_ref.at[:, cols], out_sems.at[i])

    for copy in small:
        copy.start()
    for i in range(blocks):
        load(i).start()
    for copy in small:
        copy.wait()
    route(experts, ids_s, gates_s, match_s, gate_s)
    keep = pltpu.make_async_copy(match_s, match_ref, out_sems.at[blocks])
    for i in range(blocks):
        load(i).wait()
        picked = jnp.dot(match_s[...], rows_s[i], preferred_element_type=f32)
        if i >= half:
            picked = gate_s[:, :1] * picked
        out_s[i] = picked.astype(bf16)
        store(i).start()
    keep.start()
    for i in range(blocks):
        store(i).wait()
    keep.wait()


def gather(experts, ids, gates, tokens, grad_out):
    count, width = tokens.shape
    rows = experts * CAP
    blocks = 4
    block = 2 * width // blocks
    anywhere = pl.BlockSpec(memory_space=pl.ANY)
    return pl.pallas_call(
        functools.partial(gather_kernel, experts),
        in_specs=[anywhere] * 4,
        out_specs=[anywhere] * 2,
        out_shape=[pltpu.HBM((rows, 2 * width), bf16), pltpu.HBM((rows, count), bf16)],
        scratch_shapes=[
            pltpu.VMEM(ids.shape, ids.dtype),
            pltpu.VMEM(gates.shape, gates.dtype),
            pltpu.VMEM((blocks, count, block), bf16),
            pltpu.VMEM((rows, count), bf16),
            pltpu.VMEM((rows, 128), f32),
            pltpu.VMEM((blocks, rows, block), bf16),
            pltpu.SemaphoreType.DMA((blocks + 2,)),
            pltpu.SemaphoreType.DMA((blocks + 1,)),
        ],
        name="gather",
        cost_estimate=pl.CostEstimate(
            flops=4 * rows * count * width, bytes_accessed=4 * width * (rows + count), transcendentals=0
        ),
        compiler_params=pltpu.CompilerParams(
            vmem_limit_bytes=8 * MIB + 8 * width * (rows + count)
        ),
    )(in_hbm(ids), in_hbm(gates), in_hbm(tokens), in_hbm(grad_out))


def expert_kernel(
    recv_ref, gate_a, up_a, down_a, gate_b, up_b, down_b, ret_ref, own_ref, partner_ref,
    turned_s, joined_s, down_s, first_s, fold_s, total_s, coef_s, out_s, sems, coef_sems, out_sems,
):
    hidden = gate_a.shape[0]
    blocks, _, block = out_s.shape
    width = blocks * block

    size = hidden // PIECES
    units = [(h, k, p * size, size) for h in range(2) for k in range(3) for p in range(PIECES)]
    sources = ((gate_a, up_a, down_a), (gate_b, up_b, down_b))

    def held(h, k, at, size):
        if k == 2:
            return down_s.at[h, pl.ds(at, size)]
        return joined_s.at[h, pl.ds(k * hidden + at, size)]

    def load(n):
        h, k, at, size = units[n]
        return pltpu.make_async_copy(
            sources[h][k].at[pl.ds(at, size)], held(h, k, at, size), sems.at[n]
        )

    def store(i):
        return pltpu.make_async_copy(
            out_s.at[i], ret_ref.at[:, pl.ds(i * block, block)], out_sems.at[i]
        )

    for n in range(IN_FLIGHT):
        load(n).start()

    for side in range(2):
        for i in range(blocks):
            at = i * block
            turned_s[side, at : at + block, :] = recv_ref[
                :, side * width + at : side * width + at + block
            ].T
    kept = []
    for h, coef_ref in enumerate((own_ref, partner_ref)):
        for n, (half, k, at, size) in enumerate(units):
            if half != h:
                continue
            load(n).wait()
            if n + IN_FLIGHT < len(units):
                load(n + IN_FLIGHT).start()
            for m in range(0, size, PASS):
                count = min(PASS, size - m)
                to = k * hidden + at + m
                first_s[to : to + count, :] = jnp.dot(
                    held(h, k, at, size)[m : m + count, :],
                    turned_s[k // 2],
                    preferred_element_type=f32,
                )

        step = 32

        @pl.loop(0, hidden // step)
        def _(b):
            at = pl.multiple_of(b * step, step)
            g = first_s[pl.ds(at, step), :]
            u = first_s[pl.ds(hidden + at, step), :]
            a = first_s[pl.ds(2 * hidden + at, step), :]
            s = jax.nn.sigmoid(g)
            d_pre = (a * u * s * (1.0 + g * (1.0 - s))).astype(bf16)
            d_up = (a * g * s).astype(bf16)
            coef_s[h, pl.ds(at, step), :] = d_pre
            coef_s[h, pl.ds(hidden + at, step), :] = d_up
            coef_s[h, pl.ds(2 * hidden + at, step), :] = (g * s * u).astype(bf16)

        kept.append(pltpu.make_async_copy(coef_s.at[h], coef_ref, coef_sems.at[h]))
        fold_s[...] = coef_s[h, : 2 * hidden, :].T
        for i in range(blocks):
            part = jnp.dot(
                fold_s[...],
                joined_s[h, :, i * block : (i + 1) * block],
                preferred_element_type=f32,
            )
            if h == 0:
                total_s[i] = part
            else:
                out_s[i] = (total_s[i] + part).astype(bf16)
                store(i).start()
        kept[h].start()
    for i in range(blocks):
        store(i).wait()
    for copy in kept:
        copy.wait()


def expert_terms(recv, own, partner):
    rows, width = recv.shape[0], recv.shape[1] // 2
    hidden = own[0].shape[0]
    blocks = 4
    block = width // blocks
    anywhere = pl.BlockSpec(memory_space=pl.ANY)
    vmem = pl.BlockSpec(memory_space=pltpu.VMEM)
    coef = pltpu.HBM((3 * hidden, rows), bf16)
    return pl.pallas_call(
        expert_kernel,
        in_specs=[vmem] + [anywhere] * 6,
        out_specs=[anywhere] * 3,
        out_shape=[pltpu.HBM((rows, width), bf16), coef, coef],
        scratch_shapes=[
            pltpu.VMEM((2, width, rows), bf16),
            pltpu.VMEM((2, 2 * hidden, width), bf16),
            pltpu.VMEM((2, hidden, width), bf16),
            pltpu.VMEM((3 * hidden, rows), f32),
            pltpu.VMEM((rows, 2 * hidden), bf16),
            pltpu.VMEM((blocks, rows, block), f32),
            pltpu.VMEM((2, 3 * hidden, rows), bf16),
            pltpu.VMEM((blocks, rows, block), bf16),
            pltpu.SemaphoreType.DMA((6 * PIECES,)),
            pltpu.SemaphoreType.DMA((2,)),
            pltpu.SemaphoreType.DMA((blocks,)),
        ],
        name="expert_terms",
        cost_estimate=pl.CostEstimate(
            flops=20 * rows * hidden * width,
            bytes_accessed=12 * hidden * width + 6 * rows * width,
            transcendentals=2 * rows * hidden,
        ),
        compiler_params=pltpu.CompilerParams(
            vmem_limit_bytes=min(
                8 * MIB + 12 * hidden * width + 18 * rows * width, 65408 * 1024 - 4 * rows * width
            )
        ),
    )(in_vmem(recv), *(in_hbm(w) for w in (*own, *partner)))


def weight_kernel(coef_a, coef_b, x_a, dy_a, x_b, dy_b, gate_ref, up_ref, down_ref):
    hidden = gate_ref.shape[0]
    x = jnp.concatenate([x_a[...], x_b[...]], axis=0)
    dy = jnp.concatenate([dy_a[...], dy_b[...]], axis=0)
    for k, (out, right) in enumerate(((gate_ref, x), (up_ref, x), (down_ref, dy))):
        at = slice(k * hidden, (k + 1) * hidden)
        left = jnp.concatenate([coef_a[at, :], coef_b[at, :]], axis=1)
        out[...] = jnp.dot(left, right, preferred_element_type=f32).astype(bf16)


def weight_grads(coef_a, coef_b, rows_a, rows_b):
    rows, width = rows_a.shape[0], rows_a.shape[1] // 2
    hidden = coef_a.shape[0] // 3
    block = 512
    blocks = width // block
    whole = lambda i: (0, 0)
    x_at = pl.BlockSpec((rows, block), lambda i: (0, i))
    dy_at = pl.BlockSpec((rows, block), lambda i: (0, blocks + i))
    rows_b = in_hbm(rows_b)
    return pl.pallas_call(
        weight_kernel,
        grid=(blocks,),
        in_specs=[pl.BlockSpec(coef_a.shape, whole)] * 2 + [x_at, dy_at] * 2,
        out_specs=[pl.BlockSpec((hidden, block), lambda i: (0, i))] * 3,
        out_shape=[jax.ShapeDtypeStruct((hidden, width), bf16)] * 3,
        name="weight_grads",
        cost_estimate=pl.CostEstimate(
            flops=12 * rows * hidden * width,
            bytes_accessed=6 * hidden * width + 8 * rows * width,
            transcendentals=0,
        ),
        compiler_params=pltpu.CompilerParams(vmem_limit_bytes=12 * MIB + 48 * rows * (hidden + block)),
    )(in_hbm(coef_a), in_hbm(coef_b), rows_a, rows_a, rows_b, rows_b)


def combine_kernel(turned_ref, ret_ref, out_ref, out_s, out_sems):
    blocks, _, block = out_s.shape

    def store(i):
        cols = pl.ds(i * block, block)
        return pltpu.make_async_copy(out_s.at[i], out_ref.at[:, cols], out_sems.at[i])

    for i in range(blocks):
        out_s[i] = jnp.dot(
            turned_ref[...], ret_ref[:, i * block : (i + 1) * block], preferred_element_type=f32
        ).astype(bf16)
        store(i).start()
    for i in range(blocks):
        store(i).wait()


def combine(turned, ret):
    count, rows = turned.shape
    width = ret.shape[1]
    blocks = 2
    vmem = pl.BlockSpec(memory_space=pltpu.VMEM)
    return pl.pallas_call(
        combine_kernel,
        in_specs=[vmem] * 2,
        out_specs=pl.BlockSpec(memory_space=pl.ANY),
        out_shape=pltpu.HBM((count, width), bf16),
        scratch_shapes=[
            pltpu.VMEM((blocks, count, width // blocks), bf16),
            pltpu.SemaphoreType.DMA((blocks,)),
        ],
        name="combine",
        cost_estimate=pl.CostEstimate(
            flops=2 * rows * count * width, bytes_accessed=2 * (rows + count) * width, transcendentals=0
        ),
        compiler_params=pltpu.CompilerParams(
            vmem_limit_bytes=8 * MIB + 4 * (rows + count) * width
        ),
    )(in_vmem(turned), in_vmem(ret))


def exchange(rows):
    return lax.all_to_all(rows, "ep", split_axis=0, concat_axis=0, tiled=True)


def swap(value):
    return lax.ppermute(value, "tp", [(0, 1), (1, 0)])


def local(tokens, expert_ids, gate_weights, grad_out, w_gate, w_up, w_down):
    experts = lax.axis_size("ep")
    own = (w_gate[0], w_up[0], w_down[0])
    send, match = gather(experts, expert_ids.T, gate_weights.T, tokens, grad_out)
    recv = exchange(send)
    partner = tuple(swap(w) for w in own)
    turned = match.T
    ret, coef, coef_sent = expert_terms(recv, own, partner)
    back = exchange(ret)
    coef_got, rows_got = swap(coef_sent), swap(recv)
    grads = weight_grads(coef, coef_got, recv, rows_got)
    grad_tokens = combine(turned, back)
    return (grad_tokens, *(g[None] for g in grads))


def solution(mesh):
    rows = P(("ep", "tp"), None)
    weight = P("ep", "tp", None)
    return jax.shard_map(
        local,
        mesh=mesh,
        in_specs=(rows, rows, rows, rows, weight, weight, weight),
        out_specs=(rows, weight, weight, weight),
        check_vma=False,
    )
```

```python
import functools

import jax
import jax.numpy as jnp
from jax import lax
from jax.experimental import pallas as pl
from jax.experimental.pallas import tpu as pltpu
from jax.sharding import PartitionSpec as P


CAP = 8
MIB = 1 << 20
PIECES = 1
IN_FLIGHT = 3
PASS = 192
EARLY = 128

f32 = jnp.float32
bf16 = jnp.bfloat16


def in_hbm(x):
    return pltpu.with_memory_space_constraint(x, pltpu.HBM)


def in_vmem(x):
    return pltpu.with_memory_space_constraint(x, pltpu.VMEM)


def route(experts, ids_ref, gates_ref, match_ref, gate_s):
    rows, count = match_ref.shape
    expert_at = lax.broadcasted_iota(jnp.int32, (experts, count), 0)
    member = jnp.zeros((experts, count), f32)
    for k in range(ids_ref.shape[0]):
        member += jnp.where(ids_ref[k : k + 1, :] == expert_at, 1.0, 0.0)
    earlier = jnp.where(
        lax.broadcasted_iota(jnp.int32, (count, count), 0)
        < lax.broadcasted_iota(jnp.int32, (count, count), 1),
        1.0,
        0.0,
    ).astype(bf16)
    before = jnp.dot(member.astype(bf16), earlier, preferred_element_type=f32)
    row = lax.broadcasted_iota(jnp.int32, (rows, count), 0)
    match = jnp.zeros((rows, count), f32)
    gate = jnp.zeros((rows, count), f32)
    for k in range(ids_ref.shape[0]):
        named = ids_ref[k : k + 1, :]
        place = jnp.sum(
            jnp.where(named == expert_at, before, 0.0), axis=0, keepdims=True
        ).astype(jnp.int32)
        hit = jnp.where(named < experts, named * CAP + place, -1) == row
        match = jnp.where(hit, 1.0, match)
        gate = jnp.where(hit, gates_ref[k : k + 1, :], gate)
    match_ref[...] = match.astype(bf16)
    gate_s[...] = jnp.broadcast_to(jnp.sum(gate, axis=1, keepdims=True), gate_s.shape)


def gather_kernel(
    experts, ids_ref, gates_ref, tok_ref, dy_ref, send_ref, match_ref,
    ids_s, gates_s, rows_s, match_s, gate_s, out_s, sems, out_sems,
):
    blocks, _, block = rows_s.shape
    half = blocks // 2
    small = [
        pltpu.make_async_copy(ids_ref, ids_s, sems.at[blocks]),
        pltpu.make_async_copy(gates_ref, gates_s, sems.at[blocks + 1]),
    ]

    def load(i):
        src = tok_ref if i < half else dy_ref
        cols = pl.ds(i % half * block, block)
        return pltpu.make_async_copy(src.at[:, cols], rows_s.at[i], sems.at[i])

    def store(i):
        cols = pl.ds(i * block, block)
        return pltpu.make_async_copy(out_s.at[i], send_ref.at[:, cols], out_sems.at[i])

    for copy in small:
        copy.start()
    for i in range(blocks):
        load(i).start()
    for copy in small:
        copy.wait()
    route(experts, ids_s, gates_s, match_s, gate_s)
    keep = pltpu.make_async_copy(match_s, match_ref, out_sems.at[blocks])
    for i in range(blocks):
        load(i).wait()
        picked = jnp.dot(match_s[...], rows_s[i], preferred_element_type=f32)
        if i >= half:
            picked = gate_s[:, :1] * picked
        out_s[i] = picked.astype(bf16)
        store(i).start()
    keep.start()
    for i in range(blocks):
        store(i).wait()
    keep.wait()


def gather(experts, ids, gates, tokens, grad_out):
    count, width = tokens.shape
    rows = experts * CAP
    blocks = 4
    block = 2 * width // blocks
    anywhere = pl.BlockSpec(memory_space=pl.ANY)
    return pl.pallas_call(
        functools.partial(gather_kernel, experts),
        in_specs=[anywhere] * 4,
        out_specs=[anywhere] * 2,
        out_shape=[pltpu.HBM((rows, 2 * width), bf16), pltpu.HBM((rows, count), bf16)],
        scratch_shapes=[
            pltpu.VMEM(ids.shape, ids.dtype),
            pltpu.VMEM(gates.shape, gates.dtype),
            pltpu.VMEM((blocks, count, block), bf16),
            pltpu.VMEM((rows, count), bf16),
            pltpu.VMEM((rows, 128), f32),
            pltpu.VMEM((blocks, rows, block), bf16),
            pltpu.SemaphoreType.DMA((blocks + 2,)),
            pltpu.SemaphoreType.DMA((blocks + 1,)),
        ],
        name="gather",
        cost_estimate=pl.CostEstimate(
            flops=4 * rows * count * width, bytes_accessed=4 * width * (rows + count), transcendentals=0
        ),
        compiler_params=pltpu.CompilerParams(
            vmem_limit_bytes=8 * MIB + 8 * width * (rows + count)
        ),
    )(in_hbm(ids), in_hbm(gates), in_hbm(tokens), in_hbm(grad_out))


def early_kernel(src_ref, out_ref, sem):
    copy = pltpu.make_async_copy(src_ref.at[pl.ds(0, out_ref.shape[0])], out_ref, sem)
    copy.start()
    copy.wait()


def early_rows(weight):
    width = weight.shape[1]
    return pl.pallas_call(
        early_kernel,
        in_specs=[pl.BlockSpec(memory_space=pl.ANY)],
        out_specs=pl.BlockSpec(memory_space=pltpu.VMEM),
        out_shape=pltpu.VMEM((EARLY, width), bf16),
        scratch_shapes=[pltpu.SemaphoreType.DMA],
        name="early_rows",
        cost_estimate=pl.CostEstimate(flops=0, bytes_accessed=4 * EARLY * width, transcendentals=0),
        compiler_params=pltpu.CompilerParams(vmem_limit_bytes=4 * MIB),
    )(in_hbm(weight))


def expert_kernel(
    recv_ref, early_ref, gate_a, up_a, down_a, gate_b, up_b, down_b, ret_ref, own_ref, partner_ref,
    turned_s, joined_s, down_s, first_s, fold_s, total_s, coef_s, out_s,
    sems, coef_sems, out_sems, early_sem,
):
    hidden = gate_a.shape[0]
    blocks, _, block = out_s.shape
    width = blocks * block

    size = hidden // PIECES
    units = [(h, k, p * size, size) for h in range(2) for k in range(3) for p in range(PIECES)]
    early = early_ref.shape[0]
    units[0] = (0, 0, early, size - early)
    sources = ((gate_a, up_a, down_a), (gate_b, up_b, down_b))

    def held(h, k, at, size):
        if k == 2:
            return down_s.at[h, pl.ds(at, size)]
        return joined_s.at[h, pl.ds(k * hidden + at, size)]

    def load(n):
        h, k, at, size = units[n]
        return pltpu.make_async_copy(
            sources[h][k].at[pl.ds(at, size)], held(h, k, at, size), sems.at[n]
        )

    def store(i):
        return pltpu.make_async_copy(
            out_s.at[i], ret_ref.at[:, pl.ds(i * block, block)], out_sems.at[i]
        )

    for n in range(IN_FLIGHT):
        load(n).start()
    moved = pltpu.make_async_copy(early_ref, joined_s.at[0, pl.ds(0, early)], early_sem)
    moved.start()

    for side in range(2):
        for i in range(blocks):
            at = i * block
            turned_s[side, at : at + block, :] = recv_ref[
                :, side * width + at : side * width + at + block
            ].T
    first_s[:early, :] = jnp.dot(early_ref[...], turned_s[0], preferred_element_type=f32)
    kept = []
    for h, coef_ref in enumerate((own_ref, partner_ref)):
        for n, (half, k, at, size) in enumerate(units):
            if half != h:
                continue
            load(n).wait()
            if n + IN_FLIGHT < len(units):
                load(n + IN_FLIGHT).start()
            for m in range(0, size, PASS):
                count = min(PASS, size - m)
                to = k * hidden + at + m
                first_s[to : to + count, :] = jnp.dot(
                    held(h, k, at, size)[m : m + count, :],
                    turned_s[k // 2],
                    preferred_element_type=f32,
                )

        step = 32

        @pl.loop(0, hidden // step, unroll=hidden // step)
        def _(b):
            at = pl.multiple_of(b * step, step)
            g = first_s[pl.ds(at, step), :]
            u = first_s[pl.ds(hidden + at, step), :]
            a = first_s[pl.ds(2 * hidden + at, step), :]
            s = jax.nn.sigmoid(g)
            d_pre = (a * u * s * (1.0 + g * (1.0 - s))).astype(bf16)
            d_up = (a * g * s).astype(bf16)
            coef_s[h, pl.ds(at, step), :] = d_pre
            coef_s[h, pl.ds(hidden + at, step), :] = d_up
            coef_s[h, pl.ds(2 * hidden + at, step), :] = (g * s * u).astype(bf16)

        kept.append(pltpu.make_async_copy(coef_s.at[h], coef_ref, coef_sems.at[h]))
        fold_s[...] = coef_s[h, : 2 * hidden, :].T
        if h == 0:
            moved.wait()
        for i in range(blocks):
            part = jnp.dot(
                fold_s[...],
                joined_s[h, :, i * block : (i + 1) * block],
                preferred_element_type=f32,
            )
            if h == 0:
                total_s[i] = part
            else:
                out_s[i] = (total_s[i] + part).astype(bf16)
                store(i).start()
        kept[h].start()
    for i in range(blocks):
        store(i).wait()
    for copy in kept:
        copy.wait()


def expert_terms(recv, early, own, partner):
    rows, width = recv.shape[0], recv.shape[1] // 2
    hidden = own[0].shape[0]
    blocks = 4
    block = width // blocks
    anywhere = pl.BlockSpec(memory_space=pl.ANY)
    vmem = pl.BlockSpec(memory_space=pltpu.VMEM)
    coef = pltpu.HBM((3 * hidden, rows), bf16)
    return pl.pallas_call(
        expert_kernel,
        in_specs=[vmem] * 2 + [anywhere] * 6,
        out_specs=[anywhere] * 3,
        out_shape=[pltpu.HBM((rows, width), bf16), coef, coef],
        scratch_shapes=[
            pltpu.VMEM((2, width, rows), bf16),
            pltpu.VMEM((2, 2 * hidden, width), bf16),
            pltpu.VMEM((2, hidden, width), bf16),
            pltpu.VMEM((3 * hidden, rows), f32),
            pltpu.VMEM((rows, 2 * hidden), bf16),
            pltpu.VMEM((blocks, rows, block), f32),
            pltpu.VMEM((2, 3 * hidden, rows), bf16),
            pltpu.VMEM((blocks, rows, block), bf16),
            pltpu.SemaphoreType.DMA((6 * PIECES,)),
            pltpu.SemaphoreType.DMA((2,)),
            pltpu.SemaphoreType.DMA((blocks,)),
            pltpu.SemaphoreType.DMA,
        ],
        name="expert_terms",
        cost_estimate=pl.CostEstimate(
            flops=20 * rows * hidden * width,
            bytes_accessed=12 * hidden * width + 6 * rows * width,
            transcendentals=2 * rows * hidden,
        ),
        compiler_params=pltpu.CompilerParams(
            vmem_limit_bytes=min(
                8 * MIB + 12 * hidden * width + 18 * rows * width, 65408 * 1024 - 2 * width * (2 * rows + EARLY)
            )
        ),
    )(in_vmem(recv), in_vmem(early), *(in_hbm(w) for w in (*own, *partner)))


def weight_kernel(coef_a, coef_b, x_a, dy_a, x_b, dy_b, gate_ref, up_ref, down_ref):
    hidden = gate_ref.shape[0]
    x = jnp.concatenate([x_a[...], x_b[...]], axis=0)
    dy = jnp.concatenate([dy_a[...], dy_b[...]], axis=0)
    for k, (out, right) in enumerate(((gate_ref, x), (up_ref, x), (down_ref, dy))):
        at = slice(k * hidden, (k + 1) * hidden)
        left = jnp.concatenate([coef_a[at, :], coef_b[at, :]], axis=1)
        out[...] = jnp.dot(left, right, preferred_element_type=f32).astype(bf16)


def weight_grads(coef_a, coef_b, rows_a, rows_b):
    rows, width = rows_a.shape[0], rows_a.shape[1] // 2
    hidden = coef_a.shape[0] // 3
    block = 512
    blocks = width // block
    whole = lambda i: (0, 0)
    x_at = pl.BlockSpec((rows, block), lambda i: (0, i))
    dy_at = pl.BlockSpec((rows, block), lambda i: (0, blocks + i))
    rows_b = in_hbm(rows_b)
    return pl.pallas_call(
        weight_kernel,
        grid=(blocks,),
        in_specs=[pl.BlockSpec(coef_a.shape, whole)] * 2 + [x_at, dy_at] * 2,
        out_specs=[pl.BlockSpec((hidden, block), lambda i: (0, i))] * 3,
        out_shape=[jax.ShapeDtypeStruct((hidden, width), bf16)] * 3,
        name="weight_grads",
        cost_estimate=pl.CostEstimate(
            flops=12 * rows * hidden * width,
            bytes_accessed=6 * hidden * width + 8 * rows * width,
            transcendentals=0,
        ),
        compiler_params=pltpu.CompilerParams(vmem_limit_bytes=12 * MIB + 48 * rows * (hidden + block)),
    )(in_hbm(coef_a), in_hbm(coef_b), rows_a, rows_a, rows_b, rows_b)


def combine_kernel(turned_ref, ret_ref, out_ref, out_s, out_sems):
    blocks, _, block = out_s.shape

    def store(i):
        cols = pl.ds(i * block, block)
        return pltpu.make_async_copy(out_s.at[i], out_ref.at[:, cols], out_sems.at[i])

    for i in range(blocks):
        out_s[i] = jnp.dot(
            turned_ref[...], ret_ref[:, i * block : (i + 1) * block], preferred_element_type=f32
        ).astype(bf16)
        store(i).start()
    for i in range(blocks):
        store(i).wait()


def combine(turned, ret):
    count, rows = turned.shape
    width = ret.shape[1]
    blocks = 4
    vmem = pl.BlockSpec(memory_space=pltpu.VMEM)
    return pl.pallas_call(
        combine_kernel,
        in_specs=[vmem] * 2,
        out_specs=pl.BlockSpec(memory_space=pl.ANY),
        out_shape=pltpu.HBM((count, width), bf16),
        scratch_shapes=[
            pltpu.VMEM((blocks, count, width // blocks), bf16),
            pltpu.SemaphoreType.DMA((blocks,)),
        ],
        name="combine",
        cost_estimate=pl.CostEstimate(
            flops=2 * rows * count * width, bytes_accessed=2 * (rows + count) * width, transcendentals=0
        ),
        compiler_params=pltpu.CompilerParams(
            vmem_limit_bytes=8 * MIB + 4 * (rows + count) * width
        ),
    )(in_vmem(turned), in_vmem(ret))


def exchange(rows):
    return lax.all_to_all(rows, "ep", split_axis=0, concat_axis=0, tiled=True)


def swap(value):
    return lax.ppermute(value, "tp", [(0, 1), (1, 0)])


def local(tokens, expert_ids, gate_weights, grad_out, w_gate, w_up, w_down):
    experts = lax.axis_size("ep")
    own = (w_gate[0], w_up[0], w_down[0])
    send, match = gather(experts, expert_ids.T, gate_weights.T, tokens, grad_out)
    recv = exchange(send)
    partner = tuple(swap(w) for w in own)
    turned = match.T
    early = early_rows(own[0])
    ret, coef, coef_sent = expert_terms(recv, early, own, partner)
    back = exchange(ret)
    coef_got, rows_got = swap(coef_sent), swap(recv)
    grads = weight_grads(coef, coef_got, recv, rows_got)
    grad_tokens = combine(turned, back)
    return (grad_tokens, *(g[None] for g in grads))


def solution(mesh):
    rows = P(("ep", "tp"), None)
    weight = P("ep", "tp", None)
    return jax.shard_map(
        local,
        mesh=mesh,
        in_specs=(rows, rows, rows, rows, weight, weight, weight),
        out_specs=(rows, weight, weight, weight),
        check_vma=False,
    )
```
